32 devices in a mesh: shard: 4 (over z), ctx: 2 (over x), tp: 4 (over y, core).
Axes of the slice: x: 2, y: 2, z: 4, core: 2. Of those that a mesh axis runs over, the one named last changes fastest.
Arguments:
- activations: bfloat16 [4, 1040, 768], P('shard', 'ctx'), may hold values from -6 to 6
- slot_counts: int32 [4, 2], P('shard'), may hold values from 1 to 520, as said below
- qkv_weight: bfloat16 [3, 768, 768], P(None, 'shard', 'tp'), may hold values from -0.21875 to 0.21875
- proj_weight: bfloat16 [768, 768], P('tp', 'shard'), may hold values from -3 to 3
- up_weight: bfloat16 [768, 3072], P('shard', 'tp'), may hold values from -0.21875 to 0.21875
- down_weight: bfloat16 [3072, 768], P('tp', 'shard'), may hold values from -0.109375 to 0.109375
- norm_gains: bfloat16 [2, 768], P(None, 'shard'), may hold values from 0.5 to 1.5
- row_biases: bfloat16 [4, 768], P(None, 'shard'), may hold values from -3 to 3
- head_biases: bfloat16 [2, 768], P(None, 'tp'), may hold values from -0.59765625 to 0.59765625
- hidden_bias: bfloat16 [3072], P('tp'), may hold values from -3 to 3
- cotangent: bfloat16 [4, 1040, 768], P('shard', 'ctx'), may hold values from -6 to 6
Outputs:
- layer_out: bfloat16 [4, 1040, 768], P('shard', ('ctx', 'tp'))
- input_grad: bfloat16 [4, 1040, 768], P('shard', ('ctx', 'tp'))
- qkv_weight_grad: float32 [3, 768, 768], P(None, 'shard', 'tp')
- proj_weight_grad: float32 [768, 768], P('tp', 'shard')
- up_weight_grad: float32 [768, 3072], P('shard', 'tp')
- down_weight_grad: float32 [3072, 768], P('tp', 'shard')
- norm_gains_grad: float32 [2, 768], P(None, 'shard')
- row_biases_grad: float32 [4, 768], P(None, 'shard')
- head_biases_grad: float32 [2, 768], P(None, 'tp')
- hidden_bias_grad: float32 [3072], P('tp')
The draws below stay inside these ranges and needn't reach their ends.
Inputs may be any that keep to these rules, and one draw needn't show every extreme that they name: Row b splits image b's 1025 tokens over the indices of ctx: slot_counts[b, r] of them lie in the first slots of index r's 520; each row sums to 1025; in each row one index holds exactly 520 and the others share the rest as evenly as possible.
All inputs are finite; a program needn't handle non-finite values.
Results may differ from the reference program's by a relative error of at most 0.012.
Values may be sent and summed in bfloat16 or wider, within the bound.
No kernel may reach another device: no remote copies, remote signals or barrier semaphores. Data moves between devices by JAX's collectives and lax.ppermute only.
A program may use at most 64 MiB of HBM per device.

```python
import math
import jax
import jax.numpy as jnp
from jax import lax

D = 768
HEADS = 12
HD = 64
FF = 3072
SEQ = 1025
SLOTS = 520
IMAGES = 4
N_CTX = 2


def draw_slot_counts(key, part):
    rest = SEQ - SLOTS
    others = N_CTX - 1
    base = rest // others
    extra = rest % others
    order = jnp.arange(others, dtype=jnp.int32)
    fill = (base + (order < extra).astype(jnp.int32)).astype(jnp.int32)
    full_rank = jax.random.randint(key, (IMAGES, 1), 0, N_CTX).astype(jnp.int32)
    ranks = jnp.arange(N_CTX, dtype=jnp.int32)[None, :]
    other_index = ranks - (ranks > full_rank).astype(jnp.int32)
    other_index = jnp.clip(other_index, 0, others - 1)
    spread = fill[other_index]
    return jnp.where(ranks == full_rank, SLOTS, spread).astype(jnp.int32)


def levels(own_key, shape, shards, least, high):
    loudness = 1.0
    for position, shards_of in shards:
        draws = jax.random.uniform(jax.random.fold_in(jax.random.fold_in(own_key, 6), position), (shards_of,), jnp.float32, least / len(shards), high / len(shards))
        loudness = loudness * jnp.repeat(jnp.exp(draws), shape[position] // shards_of).reshape((-1,) + (1,) * (len(shape) - 1 - position))
    return loudness


def noise(own_key, dims, scale, most, pieces=(), kind=jnp.bfloat16):
    loudness = levels(own_key, dims, pieces, -0.22, 0.18) if pieces else 1.0
    drawn = jax.random.normal(own_key, dims, jnp.float32) * scale * loudness
    return jnp.minimum(jnp.maximum(drawn, -most), most).astype(kind)


def setup_inputs(seed: int = 0) -> dict:
    arg_keys = jax.random.split(jax.random.key(seed), 12)
    return {
        "activations": noise(arg_keys[0], (IMAGES, N_CTX * SLOTS, D), 1.0, 6.0, ((0, 4), (1, 2))),
        "slot_counts": draw_slot_counts(jax.random.fold_in(arg_keys[11], 71), 0),
        "qkv_weight": noise(arg_keys[2], (3, D, D), D ** -0.5, 0.21875, ((1, 4), (2, 4))),
        "proj_weight": noise(arg_keys[3], (D, D), 4 ** -0.5, 3.0, ((0, 4), (1, 4))),
        "up_weight": noise(arg_keys[4], (D, FF), D ** -0.5, 0.21875, ((0, 4), (1, 4))),
        "down_weight": noise(arg_keys[5], (FF, D), FF ** -0.5, 0.109375, ((0, 4), (1, 4))),
        "norm_gains": jnp.clip(1.0 + 0.1 * jax.random.normal(arg_keys[6], (2, D), jnp.float32), 0.5, 1.5).astype(jnp.bfloat16),
        "row_biases": noise(arg_keys[7], (4, D), 0.5, 3.0, ((1, 4),)),
        "head_biases": noise(arg_keys[8], (2, D), 0.1, 0.59765625, ((1, 4),)),
        "hidden_bias": noise(arg_keys[9], (FF,), 0.5, 3.0, ((0, 4),)),
        "cotangent": noise(arg_keys[10], (IMAGES, N_CTX * SLOTS, D), 1.0, 6.0, ((0, 4), (1, 2))),
    }


EPS = 1e-06
NEG = -1e+30
HIGH = lax.Precision.HIGHEST

@jax.custom_vjp
def low(v):
    return lax.optimization_barrier(v.astype(jnp.bfloat16)).astype(jnp.float32)

@jax.custom_vjp
def low_back(v):
    return v

def low_keep(v):
    return (low(v), None)

def low_pass(kept, grad):
    return (grad,)

def back_keep(v):
    return (v, None)

def back_low(kept, grad):
    return (low(grad),)
low.defvjp(low_keep, low_pass)
low_back.defvjp(back_keep, back_low)

def layer_norm(values, gain, shift):
    centred = values - lax.optimization_barrier(jnp.mean(values, axis=-1, keepdims=True))
    spread = lax.optimization_barrier(jnp.mean(centred * centred, axis=-1, keepdims=True))
    return centred * lax.rsqrt(spread + EPS) * gain + shift

def matmul(left, right):
    return jnp.dot(left, right, precision=HIGH, preferred_element_type=jnp.float32)

def attention(queries, keys, values, keep):
    scale = 1.0 / math.sqrt(HD)
    scores = jnp.einsum('qhd,khd->hqk', queries, keys, precision=HIGH) * scale
    scores = low_back(scores)
    scores = jnp.where(keep[None, None, :], scores, NEG)
    probs = low(jax.nn.softmax(scores, axis=-1))
    return jnp.einsum('hqk,khd->qhd', probs, values, precision=HIGH)

def forward(act_in, keep, qkv_weight, proj_weight, up_weight, down_weight, norm_gains, row_biases, head_biases, hidden_bias):
    slot_total = act_in.shape[0]
    head_shape = (slot_total, HEADS, HD)
    normed = low(layer_norm(act_in, norm_gains[0], row_biases[0]))
    queries = low(low_back(matmul(normed, qkv_weight[0]) + head_biases[0]))
    keys = low(low_back(matmul(normed, qkv_weight[1])))
    values = low(low_back(matmul(normed, qkv_weight[2]) + head_biases[1]))
    mixed = attention(queries.reshape(head_shape), keys.reshape(head_shape), values.reshape(head_shape), keep)
    mixed = low(low_back(mixed.reshape(slot_total, D)))
    branch = low_back(matmul(mixed, proj_weight) + row_biases[2])
    middle = act_in + branch
    normed_two = low(layer_norm(middle, norm_gains[1], row_biases[1]))
    hidden = low_back(matmul(normed_two, up_weight) + hidden_bias)
    gelu_out = low(jax.nn.gelu(hidden, approximate=False))
    branch_two = low_back(matmul(gelu_out, down_weight) + row_biases[3])
    return jnp.where(keep[:, None], middle + branch_two, 0.0)

def reference(activations, slot_counts, qkv_weight, proj_weight, up_weight, down_weight, norm_gains, row_biases, head_biases, hidden_bias, cotangent):
    params = tuple((weight.astype(jnp.float32) for weight in (qkv_weight, proj_weight, up_weight, down_weight, norm_gains, row_biases, head_biases, hidden_bias)))
    slot_ids = (jnp.arange(N_CTX * SLOTS) % SLOTS).astype(jnp.int32)
    valid = jnp.repeat(slot_counts, SLOTS, axis=1) > slot_ids[None, :]

    def one_image(totals, item):
        image, keep, grad_out = item

        def local(act_in, *weights):
            return forward(act_in, keep, *weights)
        result, pull = jax.vjp(local, image.astype(jnp.float32), *params)
        grads = pull(grad_out.astype(jnp.float32))
        totals = tuple((total + grad for total, grad in zip(totals, grads[1:])))
        return (totals, (result.astype(jnp.bfloat16), grads[0].astype(jnp.bfloat16)))
    zeros = tuple((jnp.zeros(weight.shape, jnp.float32) for weight in params))
    totals, outputs = lax.scan(one_image, zeros, (activations, valid, cotangent))
    return (outputs[0], outputs[1], totals[0], totals[1], totals[2], totals[3], totals[4], totals[5], totals[6], totals[7])
```

```python
import math

import jax
import jax.numpy as jnp
from jax import lax
from jax.sharding import PartitionSpec as P

HD = 64
EPS = 1e-06
NEG = -1e30
F32 = jnp.float32
LOW = jnp.bfloat16


def norm_stats(values):
    centred = values - jnp.mean(values, axis=-1, keepdims=True)
    rate = lax.rsqrt(jnp.mean(centred * centred, axis=-1, keepdims=True) + EPS)
    return centred * rate, rate


def norm_back(grad, scaled, rate, gain):
    e = grad * gain
    inner = jnp.mean(e * scaled, axis=-1, keepdims=True)
    return rate * (e - jnp.mean(e, axis=-1, keepdims=True) - scaled * inner)


def dot(left, right, left_dim=1, right_dim=0):
    return lax.dot_general(
        left, right, (((left_dim,), (right_dim,)), ((), ())), preferred_element_type=F32
    )


def per_device(
    activations,
    slot_counts,
    qkv_weight,
    proj_weight,
    up_weight,
    down_weight,
    norm_gains,
    row_biases,
    head_biases,
    hidden_bias,
    cotangent,
):
    images, slots, width = activations.shape
    n_shard = lax.axis_size("shard")
    n_ctx = lax.axis_size("ctx")
    n_tp = lax.axis_size("tp")
    assert images == 1 and n_ctx == 2 and n_tp == 4
    part = width // n_shard
    heads_width = qkv_weight.shape[2]
    hidden_width = up_weight.shape[1]
    quarter = slots // n_tp
    shard = lax.axis_index("shard")
    ctx = lax.axis_index("ctx")
    tp = lax.axis_index("tp")

    def over_ctx(x):
        return lax.ppermute(x, "ctx", [(i, i ^ 1) for i in range(n_ctx)])

    def over_tp(x, bit):
        return lax.ppermute(x, "tp", [(i, i ^ bit) for i in range(n_tp)])

    def shift(x, k):
        return lax.ppermute(x, "shard", [(i, (i + k) % n_shard) for i in range(n_shard)])

    def pick(x, i):
        return lax.dynamic_index_in_dim(x, i, 0, keepdims=False)

    def half(x, axis, which):
        size = x.shape[axis] // 2
        return lax.dynamic_slice_in_dim(x, which * size, size, axis)

    def whole_shards(x, axis):
        mine = half(x, axis, ctx)
        held = [mine] + [shift(mine, k) for k in range(1, n_shard)]
        mine_all = jnp.stack(held[1:])
        other_all = over_ctx(mine_all)
        lower = jnp.where(ctx == 0, mine_all, other_all)
        upper = jnp.where(ctx == 0, other_all, mine_all)
        fetched = jnp.concatenate([lower, upper], axis=axis + 1)
        local = jnp.concatenate([x[None], fetched], axis=0)
        order = (shard - jnp.arange(n_shard)) % n_shard
        return jnp.take(local, order, axis=0)

    def spread_tp(x):
        far = over_tp(x, 2)
        near = over_tp(jnp.stack([x, far]), 1)
        return [x, near[0], far, near[1]]

    def sum_tp(blocks):
        near = over_tp(jnp.stack([blocks[1], blocks[3]]).astype(LOW), 1).astype(F32)
        own = blocks[0].astype(F32) + near[0]
        other = (blocks[2].astype(F32) + near[1]).astype(LOW)
        return own + over_tp(other, 2).astype(F32)

    def rows_of(x):
        cut = x.reshape(n_tp, quarter, width)
        return [pick(cut, tp ^ j) for j in range(n_tp)]

    def sum_owned(blocks, axis):
        sent = over_ctx(half(blocks, axis + 1, 1 - ctx).astype(LOW))
        mine = half(blocks, axis + 1, ctx).astype(F32) + sent.astype(F32)
        total = pick(mine, shard)
        low = mine.astype(LOW)
        for k in range(1, n_shard):
            total = total + shift(pick(low, (shard + k) % n_shard), k).astype(F32)
        other = over_ctx(total.astype(LOW)).astype(F32)
        lower = jnp.where(ctx == 0, total, other)
        upper = jnp.where(ctx == 0, other, total)
        return jnp.concatenate([lower, upper], axis=axis)

    act = activations[0]
    act_other = over_ctx(act)
    vectors = jnp.concatenate([norm_gains, row_biases], axis=0)
    vec_rows = -(-vectors.size // (heads_width * 16)) * 16
    vec_pack = jnp.pad(vectors.reshape(-1), (0, vec_rows * heads_width - vectors.size))
    first_pack = jnp.concatenate(
        [qkv_weight.reshape(3 * part, heads_width), vec_pack.reshape(vec_rows, heads_width)]
    )
    first = lax.all_gather(first_pack, "shard")
    qkv_full = (
        first[:, : 3 * part].reshape(n_shard, 3, part, heads_width).swapaxes(0, 1)
    ).reshape(3, width, heads_width)
    vec_full = first[:, 3 * part :].reshape(n_shard, -1)[:, : vectors.size]
    vec_full = (
        vec_full.reshape(n_shard, 6, part).swapaxes(0, 1).reshape(6, width).astype(F32)
    )
    gains, shifts = vec_full[:2], vec_full[2:]

    proj_own = whole_shards(proj_weight, 0).swapaxes(0, 1).reshape(heads_width, width)
    up_full = whole_shards(up_weight, 1).reshape(width, hidden_width)
    down_full = whole_shards(down_weight, 0).swapaxes(0, 1).reshape(hidden_width, width)
    proj_full = jnp.concatenate(spread_tp(proj_own), axis=0)

    slot_ids = jnp.arange(slots, dtype=jnp.int32)
    own_count = jnp.where(ctx == 0, slot_counts[0, 0], slot_counts[0, 1])
    other_count = jnp.where(ctx == 0, slot_counts[0, 1], slot_counts[0, 0])
    row_valid = (slot_ids < own_count)[:, None]
    key_valid = jnp.concatenate([slot_ids < own_count, slot_ids < other_count])

    act_in = act.astype(F32)
    both = jnp.concatenate([act_in, act_other.astype(F32)])
    scaled_one, rate_one = norm_stats(both)
    normed_low = (scaled_one * gains[0] + shifts[0]).astype(LOW)
    biases = head_biases.astype(F32)
    queries = (dot(normed_low[:slots], qkv_full[0]) + biases[0]).astype(LOW)
    keys = dot(normed_low, qkv_full[1]).astype(LOW)
    values = (dot(normed_low, qkv_full[2]) + biases[1]).astype(LOW)
    scale = 1.0 / math.sqrt(HD)
    query_heads = queries.reshape(slots, -1, HD)
    key_heads = keys.reshape(2 * slots, -1, HD)
    value_heads = values.reshape(2 * slots, -1, HD)
    scores = jnp.einsum("qhd,khd->hqk", query_heads, key_heads, preferred_element_type=F32)
    scores = jnp.where(key_valid[None, None, :], scores * scale, NEG)
    probs_low = jax.nn.softmax(scores, axis=-1).astype(LOW)
    mixed = jnp.einsum("hqk,khd->qhd", probs_low, value_heads, preferred_element_type=F32)
    mixed = mixed.reshape(slots, heads_width).astype(LOW)

    mixed_full = jnp.concatenate(spread_tp(mixed), axis=1)
    middle = act_in + dot(mixed_full, proj_full) + shifts[2]
    scaled_two, rate_two = norm_stats(middle)
    normed_two = (scaled_two * gains[1] + shifts[1]).astype(LOW)
    hidden = dot(normed_two, up_full) + hidden_bias.astype(F32)
    gelu_out, gelu_back = jax.vjp(lambda v: jax.nn.gelu(v, approximate=False), hidden)
    gelu_low = gelu_out.astype(LOW)
    grad_branch = jnp.where(row_valid, cotangent[0], jnp.zeros((), LOW))
    grad_out = grad_branch.astype(F32)
    (grad_hidden,) = gelu_back(dot(grad_branch, down_full, 1, 1))
    grad_hidden = grad_hidden.astype(LOW)
    grad_two = dot(grad_hidden, up_full, 1, 1)
    back_two = norm_back(grad_two, scaled_two, rate_two, gains[1])
    back_low = back_two.astype(LOW)
    back_mixed = dot(back_low, proj_full, 1, 1).reshape(slots, n_tp, heads_width)
    grad_mixed = sum_tp([back_mixed[:, j] for j in range(n_tp)])
    grad_mixed = (grad_mixed + dot(grad_branch, proj_own, 1, 1)).astype(LOW)

    mlp_sum = sum_tp(rows_of(dot(gelu_low, down_full).astype(LOW)))
    own_valid = rows_of(jnp.broadcast_to(row_valid, (slots, width)))[0]
    layer_out = jnp.where(own_valid, rows_of(middle)[0] + mlp_sum + shifts[3], 0.0).astype(LOW)
    back_rows = sum_tp(rows_of(back_low))
    grad_middle = rows_of(grad_out)[0] + back_rows
    attn_blocks = jnp.stack(spread_tp(grad_middle.astype(LOW)))
    grad_attn = jnp.take(attn_blocks, tp ^ jnp.arange(n_tp), axis=0).reshape(slots, width)

    down_blocks = dot(gelu_low, grad_branch, 0, 0).reshape(hidden_width, n_shard, part)
    down_grad = sum_owned(down_blocks.swapaxes(0, 1), 0)
    up_blocks = dot(normed_two, grad_hidden, 0, 0).reshape(n_shard, part, hidden_width)
    up_grad = sum_owned(up_blocks, 1)
    proj_blocks = dot(mixed, grad_attn, 0, 0).reshape(heads_width, n_shard, part)
    proj_grad = sum_owned(proj_blocks.swapaxes(0, 1), 0)

    grad_heads = grad_mixed.reshape(slots, -1, HD)
    mixed_heads = mixed.reshape(slots, -1, HD)
    inner = jnp.sum(grad_heads.astype(F32) * mixed_heads.astype(F32), axis=-1)
    grad_probs = jnp.einsum("qhd,khd->hqk", grad_heads, value_heads, preferred_element_type=F32)
    grad_scores = (probs_low.astype(F32) * (grad_probs - inner.T[:, :, None])).astype(LOW)
    grad_values = jnp.einsum("hqk,qhd->khd", probs_low, grad_heads, preferred_element_type=F32)
    grad_keys = jnp.einsum("hqk,qhd->khd", grad_scores, query_heads, preferred_element_type=F32)
    grad_queries = jnp.einsum("hqk,khd->qhd", grad_scores, key_heads, preferred_element_type=F32)
    grad_queries = (grad_queries * scale).reshape(slots, heads_width).astype(LOW)
    grad_keys = (grad_keys * scale).reshape(2 * slots, heads_width).astype(LOW)
    grad_values = grad_values.reshape(2 * slots, heads_width).astype(LOW)

    grad_other = dot(grad_keys, qkv_full[1], 1, 1) + dot(grad_values, qkv_full[2], 1, 1)
    grad_own = grad_other[:slots] + dot(grad_queries, qkv_full[0], 1, 1)
    grad_one = jnp.concatenate([grad_own, grad_other[slots:]])
    own_rows = rows_of(grad_one[:slots].astype(LOW))
    other_rows = rows_of(grad_one[slots:].astype(LOW))
    near = over_tp(jnp.stack([own_rows[1], own_rows[3], other_rows[1], other_rows[3]]), 1)
    summed = jnp.stack([own_rows[0], own_rows[2], other_rows[0], other_rows[2]]).astype(F32)
    summed = summed + near.astype(F32)
    summed_low = summed.astype(LOW)
    from_tp = over_tp(summed_low[1], 2)
    from_ctx = over_ctx(summed_low[2])
    pairs = [(i, i ^ (n_tp + 2)) for i in range(n_ctx * n_tp)]
    from_far = lax.ppermute(summed_low[3], ("ctx", "tp"), pairs)
    grad_rows = summed[0] + from_tp.astype(F32) + from_ctx.astype(F32) + from_far.astype(F32)

    qkv_grads = [
        dot(normed_low[:slots], grad_queries, 0, 0),
        dot(normed_low, grad_keys, 0, 0),
        dot(normed_low, grad_values, 0, 0),
    ]
    qkv_blocks = jnp.stack(qkv_grads).reshape(3, n_shard, part, heads_width).swapaxes(0, 1)
    qkv_grad = sum_owned(qkv_blocks, 1)

    own_scaled, own_rate = norm_stats(rows_of(act_in)[0])
    input_grad = (grad_middle + norm_back(grad_rows, own_scaled, own_rate, gains[0])).astype(LOW)

    first_tp = jnp.where(tp == 0, 1.0, 0.0)
    branch_sum = jnp.sum(grad_out, axis=0) * first_tp
    head_sums = jnp.concatenate(
        [
            jnp.sum(grad_queries.astype(F32), axis=0),
            jnp.sum(grad_values.astype(F32), axis=0),
            jnp.zeros((width - 2 * heads_width,), F32),
        ]
    )
    sums = jnp.stack(
        [
            jnp.sum(grad_one * scaled_one, axis=0),
            jnp.sum(grad_two * scaled_two, axis=0),
            jnp.sum(grad_one, axis=0),
            jnp.sum(grad_two, axis=0),
            branch_sum + jnp.sum(back_two, axis=0),
            branch_sum,
        ]
    )
    for bit in (1, 2):
        sums = sums + over_tp(sums, bit)
    own_sums = jnp.stack([jnp.sum(grad_hidden.astype(F32), axis=0), head_sums])
    sums = jnp.concatenate([sums, own_sums])
    sums = sums + over_ctx(sums)
    bit = 1
    while bit < n_shard:
        sums = sums + lax.ppermute(sums, "shard", [(i, i ^ bit) for i in range(n_shard)])
        bit *= 2
    vector_grads = lax.dynamic_slice_in_dim(sums[:6], shard * part, part, 1)
    return (
        layer_out[None],
        input_grad[None],
        qkv_grad,
        proj_grad,
        up_grad,
        down_grad,
        vector_grads[:2],
        vector_grads[2:],
        sums[7, : 2 * heads_width].reshape(2, heads_width),
        sums[6],
    )


def solution(mesh):
    placed = (
        P("shard", "ctx", None),
        P("shard", None),
        P(None, "shard", "tp"),
        P("tp", "shard"),
        P("shard", "tp"),
        P("tp", "shard"),
        P(None, "shard"),
        P(None, "shard"),
        P(None, "tp"),
        P("tp"),
        P("shard", "ctx", None),
    )
    return jax.shard_map(
        per_device,
        mesh=mesh,
        in_specs=placed,
        out_specs=(
            P("shard", ("ctx", "tp"), None),
            P("shard", ("ctx", "tp"), None),
            P(None, "shard", "tp"),
            P("tp", "shard"),
            P("shard", "tp"),
            P("tp", "shard"),
            P(None, "shard"),
            P(None, "shard"),
            P(None, "tp"),
            P("tp"),
        ),
        check_vma=False,
    )
```

```python
import math

import jax
import jax.numpy as jnp
from jax import lax
from jax.experimental import pallas as pl
from jax.experimental.pallas import tpu as pltpu
from jax.sharding import PartitionSpec as P

HD = 64
EPS = 1e-06
NEG = -1e30
F32 = jnp.float32
LOW = jnp.bfloat16
VMEM = pl.BlockSpec(memory_space=pltpu.VMEM)
SMEM = pl.BlockSpec(memory_space=pltpu.SMEM)


def shape(dims, dtype=LOW):
    return jax.ShapeDtypeStruct(dims, dtype)


def call(body, name, out, args, scalars=0, scratch=(), cost=None):
    return pl.pallas_call(
        body,
        name=name,
        out_shape=out,
        in_specs=[SMEM] * scalars + [VMEM] * (len(args) - scalars),
        out_specs=[VMEM] * len(out),
        scratch_shapes=list(scratch),
        compiler_params=pltpu.CompilerParams(vmem_limit_bytes=60 * 2**20),
        cost_estimate=cost,
    )(*args)


def cost(flops, moved, exps=0):
    return pl.CostEstimate(flops=flops, bytes_accessed=moved, transcendentals=exps)


def dot(left, right, left_dim=1, right_dim=0):
    return lax.dot_general(
        left, right, (((left_dim,), (right_dim,)), ((), ())), preferred_element_type=F32
    )


def norm_stats(values):
    centred = values - jnp.mean(values, axis=-1, keepdims=True)
    rate = lax.rsqrt(jnp.mean(centred * centred, axis=-1, keepdims=True) + EPS)
    return centred * rate, rate


def norm_back(grad, scaled, rate, gain):
    e = grad * gain
    inner = jnp.mean(e * scaled, axis=-1, keepdims=True)
    return rate * (e - jnp.mean(e, axis=-1, keepdims=True) - scaled * inner)


def own_other(counts):
    ctx = lax.axis_index("ctx")
    first, second = counts[0, 0], counts[0, 1]
    return jnp.where(ctx == 0, first, second), jnp.where(ctx == 0, second, first)


def wide(blocks):
    return jnp.concatenate(blocks, axis=1)


def to_chunks(value, ref):
    tp = lax.axis_index("tp")
    count, rows = ref.shape[0], ref.shape[1]
    for g in range(count):
        ref[tp ^ g] = value[g * rows : (g + 1) * rows].astype(ref.dtype)


def to_blocks(value, ref, row):
    n, _, part = ref.shape
    for g in range(n):
        ref[g, row : row + value.shape[0], :] = value[:, g * part : (g + 1) * part].astype(ref.dtype)


def pack_body(qkv, gains, biases, proj, up, down, first, rest, rest_half, down_half):
    ctx = lax.axis_index("ctx")
    heads_width = qkv.shape[2]
    part = qkv.shape[1]
    for k in range(3):
        first[k * heads_width : (k + 1) * heads_width, :] = qkv[k].T
    vectors = jnp.concatenate(
        [gains[...].astype(F32), biases[...].astype(F32), jnp.zeros((10, part), F32)], axis=0
    )
    first[3 * heads_width :, :] = vectors.astype(LOW)
    rest[:heads_width, :] = proj[...]
    rest[heads_width:, :] = up[...].T
    size = rest_half.shape[0]
    rest_half[...] = rest[pl.ds(pl.multiple_of(ctx * size, 16), size), :]
    size = down_half.shape[0]
    down_half[...] = down[pl.ds(pl.multiple_of(ctx * size, 16), size), :]


def assemble(own, pairs, middle, held):
    n, rows, _ = held.shape
    shard, ctx = lax.axis_index("shard"), lax.axis_index("ctx")
    held[shard] = own[...]
    for k, (mine, other) in enumerate(pairs, 1):
        step = jnp.where(ctx == 0, n - k, k)
        held[(shard + step) % n] = mine[...]
        held[(shard + n - step) % n] = other[...]
    if middle:
        far = (shard + n // 2) % n
        size = rows // 2
        held[far, pl.ds(pl.multiple_of(ctx * size, 16), size), :] = middle[0][...]
        held[far, pl.ds(pl.multiple_of((1 - ctx) * size, 16), size), :] = middle[1][...]


def assemble_body(splits, n, *refs):
    outs, held = refs[-1 - len(splits) : -1], refs[-1]
    ins = refs[: -1 - len(splits)]
    count = (n - 1) // 2
    pairs = [(ins[1 + 2 * i], ins[2 + 2 * i]) for i in range(count)]
    assemble(ins[0], pairs, ins[1 + 2 * count :], held)
    row = 0
    for size, out in zip(splits, outs):
        out[...] = wide([held[g, row : row + size, :] for g in range(n)])
        row += size


def attend_body(
    counts, act, other, first, biases, mixed_out, turned_out, scale_out, normed_own,
    normed_other, q_out, k_out, v_out, e_out, w_out,
):
    n = first.shape[0]
    slots = act.shape[0]
    hw = biases.shape[1]
    weights = wide([first[g] for g in range(n)])
    w_out[...] = weights
    vectors = weights[3 * hw :].astype(F32)
    bias = biases[...].astype(F32)
    for src, dst in ((act, normed_own), (other, normed_other)):
        scaled, _ = norm_stats(src[...].astype(F32))
        dst[...] = (scaled * vectors[0:1] + vectors[2:3]).astype(LOW)
    queries = (dot(normed_own[...], weights[:hw], 1, 1) + bias[0:1]).astype(LOW)
    q_out[...] = (queries.astype(F32) * (1.0 / math.sqrt(HD))).astype(LOW)
    for i, src in enumerate((normed_own, normed_other)):
        both = dot(src[...], weights[hw : 3 * hw], 1, 1)
        k_out[i] = both[:, :hw].astype(LOW)
        v_out[i] = (both[:, hw:] + bias[1:2]).astype(LOW)
    ids = lax.broadcasted_iota(jnp.int32, (slots, 1), 0)
    outs, scales = [], []
    for h in range(hw // HD):
        cols = slice(h * HD, (h + 1) * HD)
        query = q_out[:, cols]
        scores = [
            jnp.where(ids < count, dot(k_out[i][:, cols], query, 1, 1), NEG)
            for i, count in enumerate(own_other(counts))
        ]
        peak = jnp.maximum(*[jnp.max(s, axis=0, keepdims=True) for s in scores])
        mixed, total = 0.0, 0.0
        for i in range(2):
            e = jnp.exp(scores[i] - peak)
            total = total + jnp.sum(e, axis=0, keepdims=True)
            e_out[h, i] = e.astype(LOW)
            mixed = mixed + dot(v_out[i][:, cols], e_out[h, i], 0, 0)
        scales.append(1.0 / total)
        outs.append(mixed * scales[-1])
    turned = jnp.concatenate(outs, axis=0)
    turned_out[...] = turned
    mixed_out[...] = turned.T.astype(LOW)
    scales.append(jnp.zeros((8 - len(scales), slots), F32))
    scale_out[...] = jnp.concatenate(scales, axis=0).T


def middle_body(
    counts, act, mixed0, mixed1, mixed2, mixed3, proj0, proj1, proj2, proj3, weights, up, down,
    hidden_bias, cot, back0, back1, back2, back3, two_out, gelu_out, hidden_out, branch_out,
    low_out, middle_out, sums,
):
    slots = act.shape[0]
    vectors = weights[weights.shape[0] - 16 :, :].astype(F32)
    own, _ = own_other(counts)
    valid = lax.broadcasted_iota(jnp.int32, (slots, 1), 0) < own
    branch = jnp.where(valid, cot[...].astype(F32), 0.0)
    branch_low = branch.astype(LOW)
    branch_out[...] = branch_low
    projs = (proj0, proj1, proj2, proj3)
    middle = act[...].astype(F32) + vectors[4:5]
    for mixed, proj in zip((mixed0, mixed1, mixed2, mixed3), projs):
        middle = middle + dot(mixed[...], proj[...])
    middle_out[...] = middle
    scaled, rate = norm_stats(middle)
    two = (scaled * vectors[1:2] + vectors[3:4]).astype(LOW)
    two_out[...] = two
    hidden = dot(two, up[...], 1, 1) + hidden_bias[...].astype(F32)
    share = 0.5 * (1.0 + lax.erf(hidden * math.sqrt(0.5)))
    gelu_out[...] = (hidden * share).astype(LOW)
    slope = share + hidden * (jnp.exp(hidden * hidden * -0.5) * (1.0 / math.sqrt(2.0 * math.pi)))
    grad_hidden = (dot(branch_low, down[...], 1, 1) * slope).astype(LOW)
    hidden_out[...] = grad_hidden
    grad_two = dot(grad_hidden, up[...])
    back = norm_back(grad_two, scaled, rate, vectors[1:2])
    low = back.astype(LOW)
    low_out[...] = low
    back0[...] = dot(low, proj0[...], 1, 1) + dot(branch_low, proj0[...], 1, 1)
    for proj, out in zip(projs[1:], (back1, back2, back3)):
        out[...] = dot(low, proj[...], 1, 1).astype(LOW)
    first_tp = jnp.where(lax.axis_index("tp") == 0, 1.0, 0.0)
    branch_sum = jnp.sum(branch, axis=0, keepdims=True) * first_tp
    sums[...] = jnp.concatenate(
        [
            jnp.sum(grad_two * scaled, axis=0, keepdims=True),
            jnp.sum(grad_two, axis=0, keepdims=True),
            branch_sum + jnp.sum(back, axis=0, keepdims=True),
            branch_sum,
            jnp.sum(grad_hidden.astype(F32), axis=0, keepdims=True),
            jnp.zeros((3, sums.shape[1]), F32),
        ],
        axis=0,
    )


def ffn_grads_body(
    two, gelu, hidden, branch, low, middle, down, near, keep, own_middle, own_branch, sent, kept,
    chunks,
):
    ctx = lax.axis_index("ctx")
    to_chunks(dot(gelu[...], down[...]), chunks)
    near[0] = chunks[1].astype(LOW)
    near[1] = chunks[3].astype(LOW)
    keep[0] = chunks[0]
    keep[2] = chunks[2]
    to_chunks(low[...].astype(F32), chunks)
    near[2] = chunks[1].astype(LOW)
    near[3] = chunks[3].astype(LOW)
    keep[1] = chunks[0]
    keep[3] = chunks[2]
    to_chunks(middle[...], chunks)
    own_middle[...] = chunks[0]
    to_chunks(branch[...].astype(F32), chunks)
    own_branch[...] = chunks[0]
    down_grad = dot(gelu[...], branch[...], 0, 0)
    up_grad = dot(hidden[...], two[...], 0, 0)

    @pl.when(ctx == 0)
    def _():
        to_blocks(down_grad, kept, 0)
        to_blocks(up_grad, sent, 0)

    @pl.when(ctx == 1)
    def _():
        to_blocks(up_grad, kept, 0)
        to_blocks(down_grad, sent, 0)


def attend_back_body(
    back0, back1, back2, q, k, v, e, scales, turned, weights, act, other, sums_in,
    gq_out, gk_out, gv_out, near, keep, own_act, sums, chunks,
):
    hw = q.shape[1]
    grad_mixed = (back0[...] + back1[...].astype(F32) + back2[...].astype(F32)).astype(LOW)
    grad_mixed = grad_mixed.astype(F32)
    scaled_grads = [
        grad_mixed[:, h * HD : (h + 1) * HD] * scales[:, h : h + 1] for h in range(hw // HD)
    ]
    scaled_grad = wide(scaled_grads)
    inner = scaled_grad.T * turned[...]
    scaled_low = scaled_grad.astype(LOW)
    scale = 1.0 / math.sqrt(HD)
    gq, gk, gv = [], ([], []), ([], [])
    for h in range(hw // HD):
        cols = slice(h * HD, (h + 1) * HD)
        grad = scaled_low[:, cols]
        row = jnp.sum(inner[cols], axis=0, keepdims=True)
        gq_head = 0.0
        for i in range(2):
            gv[i].append(dot(e[h, i], grad))
            probs_grad = dot(v[i][:, cols], grad, 1, 1)
            scores_grad = (e[h, i].astype(F32) * (probs_grad - row)).astype(LOW)
            gk[i].append(dot(scores_grad, q[:, cols]))
            gq_head = gq_head + dot(k[i][:, cols], scores_grad, 0, 0)
        gq.append(gq_head * scale)
    gq_low = jnp.concatenate(gq, axis=0).astype(LOW)
    gq_out[...] = gq_low
    for i in range(2):
        gk_out[i] = wide(gk[i]).astype(LOW)
        gv_out[i] = wide(gv[i]).astype(LOW)
    gain_sum, shift_sum = 0.0, 0.0
    for i, src in enumerate((act, other)):
        grad = dot(gk_out[i], weights[hw : 2 * hw]) + dot(gv_out[i], weights[2 * hw : 3 * hw])
        if i == 0:
            grad = grad + dot(gq_low, weights[:hw], 0, 0)
        scaled, _ = norm_stats(src[...].astype(F32))
        gain_sum = gain_sum + jnp.sum(grad * scaled, axis=0, keepdims=True)
        shift_sum = shift_sum + jnp.sum(grad, axis=0, keepdims=True)
        to_chunks(grad, chunks)
        near[2 * i] = chunks[1].astype(LOW)
        near[2 * i + 1] = chunks[3].astype(LOW)
        keep[2 * i] = chunks[0]
        keep[2 * i + 1] = chunks[2]
    to_chunks(act[...].astype(F32), chunks)
    own_act[...] = chunks[0]
    ones = jnp.ones((8, q.shape[0]), LOW)
    head_q = dot(ones, gq_low, 1, 1)[0:1]
    head_v = (dot(ones, gv_out[0]) + dot(ones, gv_out[1]))[0:1]
    pad = jnp.zeros((1, sums.shape[1] - 2 * hw), F32)
    sums[...] = jnp.concatenate(
        [
            gain_sum,
            sums_in[0:1],
            shift_sum,
            sums_in[1:2],
            sums_in[2:3],
            sums_in[3:4],
            sums_in[4:5],
            wide([head_q, head_v, pad]),
        ],
        axis=0,
    )


def head_grads_body(
    gq, gk, gv, normed_own, normed_other, mixed, attn0, attn1, attn2, attn3, sent, kept, chunks
):
    ctx = lax.axis_index("ctx")
    hw = mixed.shape[1]
    to_chunks(mixed[...].astype(F32), chunks)
    proj_grad = 0.0
    for j, attn in enumerate((attn0, attn1, attn2, attn3)):
        proj_grad = proj_grad + dot(chunks[j].astype(LOW), attn[...], 0, 0)
    q_grad = dot(gq[...], normed_own[...])
    k_grad = dot(gk[0], normed_own[...], 0, 0) + dot(gk[1], normed_other[...], 0, 0)
    v_grad = dot(gv[0], normed_own[...], 0, 0) + dot(gv[1], normed_other[...], 0, 0)

    def fill(here, there):
        to_blocks(proj_grad, here, 0)
        to_blocks(q_grad, here, hw)
        to_blocks(k_grad, there, 0)
        to_blocks(v_grad, there, hw)

    @pl.when(ctx == 0)
    def _():
        fill(kept, sent)

    @pl.when(ctx == 1)
    def _():
        fill(sent, kept)


def fold_body(kept, got, own, *outs):
    n = kept.shape[0]
    shard = lax.axis_index("shard")
    own[...] = kept[shard] + got[shard].astype(F32)
    for k, out in enumerate(outs, 1):
        owner = (shard + k) % n
        out[...] = (kept[owner] + got[owner].astype(F32)).astype(LOW)


def total_body(own, *refs):
    got, total, low = refs[:-2], refs[-2], refs[-1]
    value = own[...]
    for ref in got:
        value = value + ref[...].astype(F32)
    total[...] = value
    low[...] = value.astype(LOW)


def ffn_finish_body(mine, other, up_grad, down_grad):
    first = lax.axis_index("ctx") == 0
    theirs = other[...].astype(F32)
    down_grad[...] = jnp.where(first, mine[...], theirs)
    up_grad[...] = jnp.where(first, theirs, mine[...]).T


def head_finish_body(mine, other, qkv_grad, proj_grad):
    first = lax.axis_index("ctx") == 0
    theirs = other[...].astype(F32)
    early = jnp.where(first, mine[...], theirs)
    late = jnp.where(first, theirs, mine[...])
    hw = proj_grad.shape[0]
    proj_grad[...] = early[:hw]
    qkv_grad[0] = early[hw:].T
    qkv_grad[1] = late[:hw].T
    qkv_grad[2] = late[hw:].T


def rows_body(counts, keep, near, far, own_middle, own_branch, weights, layer_out, middle_grad, attn):
    vectors = weights[weights.shape[0] - 16 :, :].astype(F32)
    own, _ = own_other(counts)
    rows = layer_out.shape[0]
    ids = lax.broadcasted_iota(jnp.int32, (rows, 1), 0) + lax.axis_index("tp") * rows
    mlp = keep[0] + near[0].astype(F32) + far[0].astype(F32)
    value = own_middle[...] + mlp + vectors[5:6]
    layer_out[...] = jnp.where(ids < own, value, 0.0).astype(LOW)
    back = keep[1] + near[2].astype(F32) + far[1].astype(F32)
    grad = own_branch[...] + back
    middle_grad[...] = grad
    attn[...] = grad.astype(LOW)


def input_body(kept, near, from_tp, from_ctx, from_far, own_act, middle_grad, weights, out):
    vectors = weights[weights.shape[0] - 16 :, :].astype(F32)
    grad = kept[0] + near[0].astype(F32) + from_tp[...].astype(F32)
    grad = grad + from_ctx[...].astype(F32) + from_far[...].astype(F32)
    scaled, rate = norm_stats(own_act[...])
    out[...] = (middle_grad[...] + norm_back(grad, scaled, rate, vectors[0:1])).astype(LOW)


def per_device(
    activations,
    slot_counts,
    qkv_weight,
    proj_weight,
    up_weight,
    down_weight,
    norm_gains,
    row_biases,
    head_biases,
    hidden_bias,
    cotangent,
):
    images, slots, width = activations.shape
    n = lax.axis_size("shard")
    n_ctx = lax.axis_size("ctx")
    n_tp = lax.axis_size("tp")
    assert images == 1 and n_ctx == 2 and n_tp == 4 and n % 2 == 0
    part = width // n
    hw = qkv_weight.shape[2]
    ff = up_weight.shape[1]
    quarter = slots // n_tp

    def over_ctx(x):
        return lax.ppermute(x, "ctx", [(i, i ^ 1) for i in range(n_ctx)])

    def over_tp(x, bit):
        return lax.ppermute(x, "tp", [(i, i ^ bit) for i in range(n_tp)])

    def shift(x, k):
        return lax.ppermute(x, "shard", [(i, (i + k) % n) for i in range(n)])

    def shift_by_ctx(x, k):
        moves = [
            (i * n_ctx + r, ((i + (k if r == 0 else n - k)) % n) * n_ctx + r)
            for i in range(n)
            for r in range(n_ctx)
        ]
        return lax.ppermute(x, ("shard", "ctx"), moves)

    def fetch(pack, pack_half):
        mine = [shift_by_ctx(pack, k) for k in range(1, (n - 1) // 2 + 1)]
        middle = shift(pack_half, n // 2)
        pairs = [x for m in mine for x in (m, over_ctx(m))]
        return [pack] + pairs + [middle, over_ctx(middle)]

    def gather_body(splits):
        def body(*refs):
            assemble_body(splits, n, *refs)

        return body

    def spread_tp(x):
        far = over_tp(x, 2)
        return [x, over_tp(x, 1), far, over_tp(far, 1)]

    act = activations[0]
    other = over_ctx(act)
    first, rest, rest_half, down_half = call(
        pack_body,
        "pack",
        [
            shape((3 * hw + 16, part)),
            shape((hw + ff, part)),
            shape(((hw + ff) // 2, part)),
            shape((ff // 2, part)),
        ],
        [qkv_weight, norm_gains, row_biases, proj_weight, up_weight, down_weight],
    )
    first = lax.all_gather(first, "shard")
    rest_parts = fetch(rest, rest_half)
    down_parts = fetch(down_weight, down_half)

    heads = hw // HD
    (mixed, turned, scales, normed_own, normed_other, q, k, v, e, weights) = call(
        attend_body,
        "attend",
        [
            shape((slots, hw)),
            shape((hw, slots), F32),
            shape((slots, 8), F32),
            shape((slots, width)),
            shape((slots, width)),
            shape((slots, hw)),
            shape((2, slots, hw)),
            shape((2, slots, hw)),
            shape((heads, 2, slots, slots)),
            shape((3 * hw + 16, width)),
        ],
        [slot_counts, act, other, first, head_biases],
        scalars=1,
        cost=cost(3_000_000_000, 12_000_000, 2_000_000),
    )
    proj, up = call(
        gather_body((hw, ff)),
        "join",
        [shape((hw, width)), shape((ff, width))],
        rest_parts,
        scratch=[pltpu.VMEM((n, hw + ff, part), LOW)],
    )
    (down,) = call(
        gather_body((ff,)),
        "join_down",
        [shape((ff, width))],
        down_parts,
        scratch=[pltpu.VMEM((n, ff, part), LOW)],
    )
    projs = spread_tp(proj)
    mixes = spread_tp(mixed)
    back0, back1, back2, back3, two, gelu, hidden, branch, low, middle, sums = call(
        middle_body,
        "middle",
        [shape((slots, hw), F32)]
        + [shape((slots, hw))] * 3
        + [shape((slots, width)), shape((slots, ff)), shape((slots, ff))]
        + [shape((slots, width))] * 2
        + [shape((slots, width), F32), shape((8, width), F32)],
        [slot_counts, act, *mixes, *projs, weights, up, down, hidden_bias.reshape(1, ff)]
        + [cotangent[0]],
        scalars=1,
        cost=cost(4_000_000_000, 16_000_000, 1_000_000),
    )
    back1 = over_tp(back1, 1)
    back2 = (back2.astype(F32) + over_tp(back3, 1).astype(F32)).astype(LOW)
    back2 = over_tp(back2, 2)
    near, keep, own_middle, own_branch, sent, kept = call(
        ffn_grads_body,
        "ffn_grads",
        [
            shape((4, quarter, width)),
            shape((4, quarter, width), F32),
            shape((quarter, width), F32),
            shape((quarter, width), F32),
            shape((n, ff, part)),
            shape((n, ff, part), F32),
        ],
        [two, gelu, hidden, branch, low, middle, down],
        scratch=[pltpu.VMEM((n_tp, quarter, width), F32)],
        cost=cost(2_000_000_000, 14_000_000),
    )

    def owned(sent, kept):
        rows = kept.shape[1]
        own, *outs = call(
            fold_body,
            "fold",
            [shape((rows, part), F32)] + [shape((rows, part))] * (n - 1),
            [kept, over_ctx(sent)],
        )
        got = [shift(x, k) for k, x in enumerate(outs, 1)]
        total, low = call(
            total_body, "total", [shape((rows, part), F32), shape((rows, part))], [own, *got]
        )
        return [total, over_ctx(low)]

    ffn_totals = owned(sent, kept)
    near = over_tp(near, 1)
    far = jnp.stack(
        [
            (keep[2] + near[1].astype(F32)).astype(LOW),
            (keep[3] + near[3].astype(F32)).astype(LOW),
        ]
    )
    far = over_tp(far, 2)
    layer_out, middle_grad, attn = call(
        rows_body,
        "rows",
        [shape((quarter, width)), shape((quarter, width), F32), shape((quarter, width))],
        [slot_counts, keep, near, far, own_middle, own_branch, weights],
        scalars=1,
    )
    attns = spread_tp(attn)

    gq, gk, gv, near, keep, own_act, sums = call(
        attend_back_body,
        "attend_back",
        [
            shape((hw, slots)),
            shape((2, slots, hw)),
            shape((2, slots, hw)),
            shape((4, quarter, width)),
            shape((4, quarter, width), F32),
            shape((quarter, width), F32),
            shape((8, width), F32),
        ],
        [back0, back1, back2, q, k, v, e, scales, turned, weights, act, other, sums],
        scratch=[pltpu.VMEM((n_tp, quarter, width), F32)],
        cost=cost(4_000_000_000, 16_000_000),
    )
    near = over_tp(near, 1)
    sent, kept = call(
        head_grads_body,
        "head_grads",
        [shape((n, 2 * hw, part)), shape((n, 2 * hw, part), F32)],
        [gq, gk, gv, normed_own, normed_other, mixed, *attns],
        scratch=[pltpu.VMEM((n_tp, quarter, hw), F32)],
        cost=cost(1_000_000_000, 6_000_000),
    )
    head_totals = owned(sent, kept)
    from_tp = over_tp((keep[1] + near[1].astype(F32)).astype(LOW), 2)
    from_ctx = over_ctx((keep[2] + near[2].astype(F32)).astype(LOW))
    pairs = [(i, i ^ (n_tp + 2)) for i in range(n_ctx * n_tp)]
    from_far = (keep[3] + near[3].astype(F32)).astype(LOW)
    from_far = lax.ppermute(from_far, ("ctx", "tp"), pairs)
    (input_grad,) = call(
        input_body,
        "input",
        [shape((quarter, width))],
        [keep, near, from_tp, from_ctx, from_far, own_act, middle_grad, weights],
    )
    up_grad, down_grad = call(
        ffn_finish_body, "ffn_finish", [shape((part, ff), F32), shape((ff, part), F32)], ffn_totals
    )
    qkv_grad, proj_grad = call(
        head_finish_body,
        "head_finish",
        [shape((3, part, hw), F32), shape((hw, part), F32)],
        head_totals,
    )

    shared = sums[:6]
    for bit in (1, 2):
        shared = shared + over_tp(shared, bit)
    sums = jnp.concatenate([shared, sums[6:]])
    sums = sums + over_ctx(sums)
    bit = 1
    while bit < n:
        sums = sums + lax.ppermute(sums, "shard", [(i, i ^ bit) for i in range(n)])
        bit *= 2
    vector_grads = lax.dynamic_slice_in_dim(sums[:6], lax.axis_index("shard") * part, part, 1)
    return (
        layer_out[None],
        input_grad[None],
        qkv_grad,
        proj_grad,
        up_grad,
        down_grad,
        vector_grads[:2],
        vector_grads[2:],
        sums[7, : 2 * hw].reshape(2, hw),
        sums[6],
    )


def solution(mesh):
    placed = (
        P("shard", "ctx", None),
        P("shard", None),
        P(None, "shard", "tp"),
        P("tp", "shard"),
        P("shard", "tp"),
        P("tp", "shard"),
        P(None, "shard"),
        P(None, "shard"),
        P(None, "tp"),
        P("tp"),
        P("shard", "ctx", None),
    )
    return jax.shard_map(
        per_device,
        mesh=mesh,
        in_specs=placed,
        out_specs=(
            P("shard", ("ctx", "tp"), None),
            P("shard", ("ctx", "tp"), None),
            P(None, "shard", "tp"),
            P("tp", "shard"),
            P("shard", "tp"),
            P("tp", "shard"),
            P(None, "shard"),
            P(None, "shard"),
            P(None, "tp"),
            P("tp"),
        ),
        check_vma=False,
    )
```

```python
import math

import jax
import jax.numpy as jnp
from jax import lax
from jax.experimental import pallas as pl
from jax.experimental.pallas import tpu as pltpu
from jax.sharding import PartitionSpec as P

HD = 64
EPS = 1e-06
NEG = -1e30
F32 = jnp.float32
LOW = jnp.bfloat16
VMEM = pl.BlockSpec(memory_space=pltpu.VMEM)
SMEM = pl.BlockSpec(memory_space=pltpu.SMEM)


def shape(dims, dtype=LOW):
    return jax.ShapeDtypeStruct(dims, dtype)


def call(body, name, out, args, scalars=0, scratch=(), cost=None):
    return pl.pallas_call(
        body,
        name=name,
        out_shape=out,
        in_specs=[SMEM] * scalars + [VMEM] * (len(args) - scalars),
        out_specs=[VMEM] * len(out),
        scratch_shapes=list(scratch),
        compiler_params=pltpu.CompilerParams(vmem_limit_bytes=24 * 2**20),
        cost_estimate=cost,
    )(*args)


def cost(flops, moved, exps=0):
    return pl.CostEstimate(flops=flops, bytes_accessed=moved, transcendentals=exps)


def dot(left, right, left_dim=1, right_dim=0):
    return lax.dot_general(
        left, right, (((left_dim,), (right_dim,)), ((), ())), preferred_element_type=F32
    )


def norm_stats(values):
    centred = values - jnp.mean(values, axis=-1, keepdims=True)
    rate = lax.rsqrt(jnp.mean(centred * centred, axis=-1, keepdims=True) + EPS)
    return centred * rate, rate


def norm_back(grad, scaled, rate, gain):
    e = grad * gain
    inner = jnp.mean(e * scaled, axis=-1, keepdims=True)
    return rate * (e - jnp.mean(e, axis=-1, keepdims=True) - scaled * inner)


def own_other(counts):
    ctx = lax.axis_index("ctx")
    first, second = counts[0, 0], counts[0, 1]
    return jnp.where(ctx == 0, first, second), jnp.where(ctx == 0, second, first)


def wide(blocks):
    return jnp.concatenate(blocks, axis=1)


def to_chunks(value, ref):
    tp = lax.axis_index("tp")
    count = ref.shape[0]
    rows = value.shape[0] // count
    for g in range(count):
        ref[tp ^ g, :rows, :] = value[g * rows : (g + 1) * rows].astype(ref.dtype)


def folded_rows(rows):
    return (rows // 2 + 7) // 8 * 8


def fold_rows(value):
    top = folded_rows(value.shape[0])
    rest = value[top:]
    pad = jnp.zeros((top - rest.shape[0], value.shape[1]), value.dtype)
    if pad.shape[0]:
        rest = jnp.concatenate([rest, pad], axis=0)
    return wide([value[:top], rest])


def unfold_rows(value, rows):
    cols = value.shape[1] // 2
    return jnp.concatenate([value[:, :cols], value[: rows - value.shape[0], cols:]], axis=0)


def pack_body(qkv, gains, biases, proj, act, pack, pack_half, act_half):
    ctx = lax.axis_index("ctx")
    part, hw = qkv.shape[1], qkv.shape[2]
    width = pack.shape[1]
    pack[:part, :] = wide([qkv[0], qkv[1], qkv[2], proj[...].T])
    spare = pack.shape[0] - part
    vectors = jnp.concatenate(
        [gains[...].astype(F32), biases[...].astype(F32), jnp.zeros((spare - 6, part), F32)],
        axis=0,
    )
    pack[part:, :] = wide([vectors, jnp.zeros((spare, width - part), F32)]).astype(LOW)
    size = pack_half.shape[0]
    pack_half[...] = pack[pl.ds(pl.multiple_of(ctx * size, 16), size), :]
    size = act_half.shape[1]
    core = lax.axis_index("tp") % 2
    act_half[...] = act[:, pl.ds(pl.multiple_of(core * size, 128), size)]


def assemble(parts, held):
    n, rows, _ = held.shape
    shard, ctx = lax.axis_index("shard"), lax.axis_index("ctx")
    held[shard] = parts[0][...]
    for k in range(1, (n - 1) // 2 + 1):
        step = jnp.where(ctx == 0, n - k, k)
        held[(shard + step) % n] = parts[2 * k - 1][...]
        held[(shard + n - step) % n] = parts[2 * k][...]
    far = (shard + n // 2) % n
    size = rows // 2
    held[far, pl.ds(pl.multiple_of(ctx * size, 8), size), :] = parts[-2][...]
    held[far, pl.ds(pl.multiple_of((1 - ctx) * size, 8), size), :] = parts[-1][...]


def join_body(n, *refs):
    parts, (weights, proj, vectors, held) = refs[:-4], refs[-4:]
    assemble(parts, held)
    part = weights.shape[0] // n
    for g in range(n):
        weights[g * part : (g + 1) * part, :] = held[g, :part, :]
    vectors[...] = wide([held[g, part : part + 16, :part].astype(F32) for g in range(n)])[:8]
    cols = weights.shape[1] // 4
    half = weights.shape[0] // 2
    proj[...] = wide([weights[:half, 3 * cols :], weights[half:, 3 * cols :]])


def attend_body(
    counts, act, half_far, half_near, weights, vectors, biases, mixed_out, turned_out, scale_out,
    other, normed_own, normed_other, q_out, k_out, v_out, e_out,
):
    slots = act.shape[0]
    hw = biases.shape[1]
    core = lax.axis_index("tp") % 2
    size = half_far.shape[1]
    other[:, pl.ds(pl.multiple_of(core * size, 128), size)] = half_far[...]
    other[:, pl.ds(pl.multiple_of((1 - core) * size, 128), size)] = half_near[...]
    bias = biases[...].astype(F32)
    for src, dst in ((act, normed_own), (other, normed_other)):
        scaled, _ = norm_stats(src[...].astype(F32))
        dst[...] = (scaled * vectors[0:1] + vectors[2:3]).astype(LOW)
    queries = (dot(normed_own[...], weights[:, :hw]) + bias[0:1]).astype(LOW)
    q_out[...] = (queries.astype(F32) * (1.0 / math.sqrt(HD))).astype(LOW)
    for i, src in enumerate((normed_own, normed_other)):
        both = dot(src[...], weights[:, hw : 3 * hw])
        k_out[i] = both[:, :hw].astype(LOW)
        v_out[i] = (both[:, hw:] + bias[1:2]).astype(LOW)
    ids = lax.broadcasted_iota(jnp.int32, (slots, 1), 0)
    outs, scales = [], []
    for h in range(hw // HD):
        cols = slice(h * HD, (h + 1) * HD)
        query = q_out[:, cols]
        scores = [
            jnp.where(ids < count, dot(k_out[i][:, cols], query, 1, 1), NEG)
            for i, count in enumerate(own_other(counts))
        ]
        peak = jnp.maximum(*[jnp.max(s, axis=0, keepdims=True) for s in scores])
        mixed, total = 0.0, 0.0
        for i in range(2):
            e = jnp.exp(scores[i] - peak)
            total = total + jnp.sum(e, axis=0, keepdims=True)
            e_out[h, i] = e.astype(LOW)
            mixed = mixed + dot(v_out[i][:, cols], e_out[h, i], 0, 0)
        scales.append(1.0 / total)
        outs.append(mixed * scales[-1])
    turned = jnp.concatenate(outs, axis=0)
    turned_out[...] = turned
    mixed_out[...] = fold_rows(turned.T).astype(LOW)
    scales.append(jnp.zeros((8 - len(scales), slots), F32))
    scale_out[...] = jnp.concatenate(scales, axis=0).T


def middle_body(n, *refs):
    (counts, act, *rest) = refs
    mixes, projs, rest = rest[:4], rest[4:8], rest[8:]
    vectors, hidden_bias, cot, *rest = rest
    count = n + (n % 2 == 0)
    ups, downs, rest = rest[:count], rest[count : 2 * count], rest[2 * count :]
    (back0, back1, back2, back3, two_out, gelu_out, hidden_out, branch_out, low_out, middle_out,
     down_out, sums, held, proj) = rest
    slots = act.shape[0]
    width = act.shape[1]
    own, _ = own_other(counts)
    valid = lax.broadcasted_iota(jnp.int32, (slots, 1), 0) < own
    branch = jnp.where(valid, cot[...].astype(F32), 0.0)
    branch_low = branch.astype(LOW)
    branch_out[...] = branch_low
    top, bottom = 0.0, 0.0
    for j, (mixed, packed) in enumerate(zip(mixes, projs)):
        cols = packed.shape[1] // 2
        half = packed.shape[0]
        proj[j, :half, :] = packed[:, :cols]
        proj[j, half:, :] = packed[:, cols:]
        top = top + dot(mixed[:, :cols], proj[j], 1, 1)
        bottom = bottom + dot(mixed[:, cols:], proj[j], 1, 1)
    rows = slots - top.shape[0]
    middle = jnp.concatenate([top, bottom[:rows]], axis=0) + act[...].astype(F32) + vectors[4:5]
    middle_out[...] = middle
    scaled, rate = norm_stats(middle)
    two = (scaled * vectors[1:2] + vectors[3:4]).astype(LOW)
    two_out[...] = two
    assemble(downs, held)
    down_out[...] = held[...].reshape(width, -1)
    assemble(ups, held)
    up = held[...].reshape(width, -1)
    hidden = dot(two, up) + hidden_bias[...].astype(F32)
    share = 0.5 * (1.0 + lax.erf(hidden * math.sqrt(0.5)))
    gelu_out[...] = (hidden * share).astype(LOW)
    slope = share + hidden * (jnp.exp(hidden * hidden * -0.5) * (1.0 / math.sqrt(2.0 * math.pi)))
    grad_hidden = (dot(branch_low, down_out[...]) * slope).astype(LOW)
    hidden_out[...] = grad_hidden
    grad_two = dot(grad_hidden, up, 1, 1)
    back = norm_back(grad_two, scaled, rate, vectors[1:2])
    low = back.astype(LOW)
    low_out[...] = low
    back0[...] = fold_rows(dot(low, proj[0]) + dot(branch_low, proj[0]))
    for j, out in enumerate((back1, back2, back3), 1):
        out[...] = fold_rows(dot(low, proj[j])).astype(LOW)
    first_tp = jnp.where(lax.axis_index("tp") == 0, 1.0, 0.0)
    branch_sum = jnp.sum(branch, axis=0, keepdims=True) * first_tp
    sums[...] = jnp.concatenate(
        [
            jnp.sum(grad_two * scaled, axis=0, keepdims=True),
            jnp.sum(grad_two, axis=0, keepdims=True),
            branch_sum + jnp.sum(back, axis=0, keepdims=True),
            branch_sum,
            jnp.sum(grad_hidden.astype(F32), axis=0, keepdims=True),
            jnp.zeros((3, sums.shape[1]), F32),
        ],
        axis=0,
    )


def ffn_grads_body(two, gelu, hidden, branch, down, sent, kept):
    ctx = lax.axis_index("ctx")
    down_grad = dot(branch[...], gelu[...], 0, 0)
    up_grad = dot(two[...], hidden[...], 0, 0)

    @pl.when(ctx == 0)
    def _():
        kept[...] = down_grad
        sent[...] = up_grad.astype(LOW)

    @pl.when(ctx == 1)
    def _():
        kept[...] = up_grad
        sent[...] = down_grad.astype(LOW)


def ffn_rows_body(gelu, branch, low, middle, down, near, keep, own_middle, own_branch, chunks):
    rows = own_middle.shape[0]
    chunks[:, rows - 2 :, :] = jnp.zeros_like(chunks[:, rows - 2 :, :])
    to_chunks(dot(gelu[...], down[...], 1, 1), chunks)
    near[0] = chunks[1].astype(LOW)
    near[1] = chunks[3].astype(LOW)
    keep[0] = chunks[0]
    keep[2] = chunks[2]
    to_chunks(low[...].astype(F32), chunks)
    near[2] = chunks[1].astype(LOW)
    near[3] = chunks[3].astype(LOW)
    keep[1] = chunks[0]
    keep[3] = chunks[2]
    to_chunks(middle[...], chunks)
    own_middle[...] = chunks[0, :rows, :]
    to_chunks(branch[...].astype(F32), chunks)
    own_branch[...] = chunks[0, :rows, :]


def attend_back_body(
    back0, back1, back2, q, k, v, e, scales, turned, weights, act, other, sums_in,
    own_out, other_out, near, keep, own_act, sums, chunks,
):
    slots, hw = q.shape
    grad_mixed = back0[...] + back1[...].astype(F32) + back2[...].astype(F32)
    grad_mixed = unfold_rows(grad_mixed, slots).astype(LOW).astype(F32)
    scaled_grads = [
        grad_mixed[:, h * HD : (h + 1) * HD] * scales[:, h : h + 1] for h in range(hw // HD)
    ]
    scaled_grad = wide(scaled_grads)
    inner = scaled_grad.T * turned[...]
    scaled_low = scaled_grad.astype(LOW)
    scale = 1.0 / math.sqrt(HD)
    gq, gk, gv = [], ([], []), ([], [])
    for h in range(hw // HD):
        cols = slice(h * HD, (h + 1) * HD)
        grad = scaled_low[:, cols]
        row = jnp.sum(inner[cols], axis=0, keepdims=True)
        gq_head = 0.0
        for i in range(2):
            gv[i].append(dot(e[h, i], grad))
            probs_grad = dot(v[i][:, cols], grad, 1, 1)
            scores_grad = (e[h, i].astype(F32) * (probs_grad - row)).astype(LOW)
            gk[i].append(dot(scores_grad, q[:, cols]))
            gq_head = gq_head + dot(k[i][:, cols], scores_grad, 0, 0)
        gq.append(gq_head * scale)
    gq = jnp.concatenate(gq, axis=0).T
    own_out[...] = wide([gq, *gk[0], *gv[0]]).astype(LOW)
    other_out[...] = wide([*gk[1], *gv[1]]).astype(LOW)
    rows = own_act.shape[0]
    chunks[:, rows - 2 :, :] = jnp.zeros_like(chunks[:, rows - 2 :, :])
    gain_sum, shift_sum = 0.0, 0.0
    for i, src in enumerate((act, other)):
        if i == 0:
            grad = dot(own_out[...], weights[:, : 3 * hw], 1, 1)
        else:
            grad = dot(other_out[...], weights[:, hw : 3 * hw], 1, 1)
        scaled, _ = norm_stats(src[...].astype(F32))
        gain_sum = gain_sum + jnp.sum(grad * scaled, axis=0, keepdims=True)
        shift_sum = shift_sum + jnp.sum(grad, axis=0, keepdims=True)
        to_chunks(grad, chunks)
        near[2 * i] = chunks[1].astype(LOW)
        near[2 * i + 1] = chunks[3].astype(LOW)
        keep[2 * i] = chunks[0]
        keep[2 * i + 1] = chunks[2]
    to_chunks(act[...].astype(F32), chunks)
    own_act[...] = chunks[0, :rows, :]
    ones = jnp.ones((8, slots), LOW)
    own_sums = dot(ones, own_out[...])[0:1]
    other_sums = dot(ones, other_out[...])[0:1]
    head_v = own_sums[:, 2 * hw :] + other_sums[:, hw:]
    pad = jnp.zeros((1, sums.shape[1] - 2 * hw), F32)
    sums[...] = jnp.concatenate(
        [
            gain_sum,
            sums_in[0:1],
            shift_sum,
            sums_in[1:2],
            sums_in[2:3],
            sums_in[3:4],
            sums_in[4:5],
            wide([own_sums[:, :hw], head_v, pad]),
        ],
        axis=0,
    )


def head_grads_body(
    own, other, normed_own, normed_other, mixed, attn0, attn1, attn2, attn3, sent, kept, chunks
):
    ctx = lax.axis_index("ctx")
    hw = own.shape[1] // 3
    to_chunks(unfold_rows(mixed[...].astype(F32), own.shape[0]), chunks)
    proj_grad = 0.0
    for j, attn in enumerate((attn0, attn1, attn2, attn3)):
        proj_grad = proj_grad + dot(attn[...], chunks[j].astype(LOW), 0, 0)
    from_own = dot(normed_own[...], own[...], 0, 0)
    from_other = dot(normed_other[...], other[...], 0, 0)
    k_grad = from_own[:, hw : 2 * hw] + from_other[:, :hw]
    v_grad = from_own[:, 2 * hw :] + from_other[:, hw:]
    early = wide([from_own[:, :hw], k_grad])
    late = wide([v_grad, proj_grad])

    @pl.when(ctx == 0)
    def _():
        kept[...] = early
        sent[...] = late.astype(LOW)

    @pl.when(ctx == 1)
    def _():
        kept[...] = late
        sent[...] = early.astype(LOW)


def fold_body(n, kept, got, own, *outs):
    shard = lax.axis_index("shard")
    rows = own.shape[0]

    def summed(owner):
        at = pl.ds(pl.multiple_of(owner * rows, 16), rows)
        return kept[at, :] + got[at, :].astype(F32)

    own[...] = summed(shard)
    for k, out in enumerate(outs, 1):
        out[...] = summed((shard + k) % n).astype(LOW)


def total_body(own, *refs):
    got, total, low = refs[:-2], refs[-2], refs[-1]
    value = own[...]
    for ref in got:
        value = value + ref[...].astype(F32)
    total[...] = value
    low[...] = value.astype(LOW)


def ffn_finish_body(mine, other, up_grad, down_grad):
    first = lax.axis_index("ctx") == 0
    theirs = other[...].astype(F32)
    down_grad[...] = jnp.where(first, mine[...], theirs)
    up_grad[...] = jnp.where(first, theirs, mine[...])


def head_finish_body(mine, other, qkv_grad, proj_grad):
    first = lax.axis_index("ctx") == 0
    theirs = other[...].astype(F32)
    early = jnp.where(first, mine[...], theirs)
    late = jnp.where(first, theirs, mine[...])
    hw = early.shape[1] // 2
    qkv_grad[0] = early[:, :hw]
    qkv_grad[1] = early[:, hw:]
    qkv_grad[2] = late[:, :hw]
    proj_grad[...] = late[:, hw:].T


def rows_body(counts, keep, near, far, own_middle, own_branch, vectors, layer_out, middle_grad, attn):
    own, _ = own_other(counts)
    rows = layer_out.shape[0]
    ids = lax.broadcasted_iota(jnp.int32, (rows, 1), 0) + lax.axis_index("tp") * rows
    mlp = keep[0] + near[0].astype(F32) + far[0].astype(F32)
    value = own_middle[...] + mlp[:rows] + vectors[5:6]
    layer_out[...] = jnp.where(ids < own, value, 0.0).astype(LOW)
    back = keep[1] + near[2].astype(F32) + far[1].astype(F32)
    grad = own_branch[...] + back[:rows]
    middle_grad[...] = grad
    attn[...] = grad.astype(LOW)


def halfway_body(keep, near, *outs):
    for out, (i, j) in zip(outs, PAIRS[len(outs)]):
        out[...] = (keep[i] + near[j].astype(F32)).astype(LOW).reshape(out.shape)


def input_body(kept, near, from_tp, from_ctx, from_far, own_act, middle_grad, vectors, out):
    rows = out.shape[0]
    grad = kept[0] + near[0].astype(F32) + from_tp[...].astype(F32)
    grad = grad + from_ctx[...].astype(F32) + from_far[...].astype(F32)
    scaled, rate = norm_stats(own_act[...])
    back = norm_back(grad[:rows], scaled, rate, vectors[0:1])
    out[...] = (middle_grad[...] + back).astype(LOW)


PAIRS = {3: ((1, 1), (2, 2), (3, 3))}


def per_device(
    activations,
    slot_counts,
    qkv_weight,
    proj_weight,
    up_weight,
    down_weight,
    norm_gains,
    row_biases,
    head_biases,
    hidden_bias,
    cotangent,
):
    images, slots, width = activations.shape
    n = lax.axis_size("shard")
    n_ctx = lax.axis_size("ctx")
    n_tp = lax.axis_size("tp")
    assert images == 1 and n_ctx == 2 and n_tp == 4 and n % 2 == 0
    part = width // n
    hw = qkv_weight.shape[2]
    ff = up_weight.shape[1]
    quarter = slots // n_tp
    padded = (quarter + 7) // 8 * 8
    fold = folded_rows(slots)
    heads = hw // HD
    ctx = lax.axis_index("ctx")

    def over_ctx(x):
        return lax.ppermute(x, "ctx", [(i, i ^ 1) for i in range(n_ctx)])

    def over_tp(x, bit):
        return lax.ppermute(x, "tp", [(i, i ^ bit) for i in range(n_tp)])

    def shift(x, k):
        return lax.ppermute(x, "shard", [(i, (i + k) % n) for i in range(n)])

    def shift_by_ctx(x, k):
        moves = [
            (i * n_ctx + r, ((i + (k if r == 0 else n - k)) % n) * n_ctx + r)
            for i in range(n)
            for r in range(n_ctx)
        ]
        return lax.ppermute(x, ("shard", "ctx"), moves)

    def fetch(pack, pack_half):
        mine = [shift_by_ctx(pack, k) for k in range(1, (n - 1) // 2 + 1)]
        middle = shift(pack_half, n // 2)
        pairs = [x for m in mine for x in (m, over_ctx(m))]
        return [pack] + pairs + [middle, over_ctx(middle)]

    def with_n(body):
        def run(*refs):
            body(n, *refs)

        return run

    def spread_tp(x):
        far = over_tp(x, 2)
        return [x, over_tp(x, 1), far, over_tp(far, 1)]

    def row_half(x):
        size = x.shape[0] // 2
        return lax.dynamic_slice_in_dim(x, ctx * size, size, 0)

    act = activations[0]
    rows = -(-(part + 6) // 32) * 32
    pack, pack_half, act_half = call(
        pack_body,
        "pack",
        [shape((rows, width)), shape((rows // 2, width)), shape((slots, width // 2))],
        [qkv_weight, norm_gains, row_biases, proj_weight, act],
    )
    half_far = over_ctx(act_half)
    half_near = over_tp(half_far, 1)
    pack_parts = fetch(pack, pack_half)
    down_turned = down_weight.T
    up_late, down_late, _ = lax.optimization_barrier((up_weight, down_turned, pack_parts[1]))
    up_parts = fetch(up_late, row_half(up_late))
    down_late, _ = lax.optimization_barrier((down_late, up_parts[1]))
    down_parts = fetch(down_late, row_half(down_late))

    weights, proj, vectors = call(
        with_n(join_body),
        "join",
        [shape((width, width)), shape((width // 2, 2 * hw)), shape((8, width), F32)],
        pack_parts,
        scratch=[pltpu.VMEM((n, rows, width), LOW)],
    )
    (mixed, turned, scales, other, normed_own, normed_other, q, k, v, e) = call(
        attend_body,
        "attend",
        [
            shape((fold, 2 * hw)),
            shape((hw, slots), F32),
            shape((slots, 8), F32),
            shape((slots, width)),
            shape((slots, width)),
            shape((slots, width)),
            shape((slots, hw)),
            shape((2, slots, hw)),
            shape((2, slots, hw)),
            shape((heads, 2, slots, slots)),
        ],
        [slot_counts, act, half_far, half_near, weights, vectors, head_biases],
        scalars=1,
        cost=cost(3_000_000_000, 12_000_000, 2_000_000),
    )
    projs = spread_tp(proj)
    mixes = spread_tp(mixed)
    (back0, back1, back2, back3, two, gelu, hidden, branch, low, middle, down, sums) = call(
        with_n(middle_body),
        "middle",
        [shape((fold, 2 * hw), F32)]
        + [shape((fold, 2 * hw))] * 3
        + [shape((slots, width)), shape((slots, ff)), shape((slots, ff))]
        + [shape((slots, width))] * 2
        + [shape((slots, width), F32), shape((width, ff)), shape((8, width), F32)],
        [slot_counts, act, *mixes, *projs, vectors, hidden_bias.reshape(1, ff), cotangent[0]]
        + up_parts
        + down_parts,
        scalars=1,
        scratch=[pltpu.VMEM((n, part, ff), LOW), pltpu.VMEM((n_tp, width, hw), LOW)],
        cost=cost(4_000_000_000, 16_000_000, 1_000_000),
    )
    back1 = over_tp(back1, 1)
    back2 = (back2.astype(F32) + over_tp(back3, 1).astype(F32)).astype(LOW)
    back2 = over_tp(back2, 2)
    sent, kept = call(
        ffn_grads_body,
        "ffn_grads",
        [shape((width, ff)), shape((width, ff), F32)],
        [two, gelu, hidden, branch, down],
        cost=cost(1_300_000_000, 7_000_000),
    )
    near, keep, own_middle, own_branch = call(
        ffn_rows_body,
        "ffn_rows",
        [
            shape((4, padded, width)),
            shape((4, padded, width), F32),
            shape((quarter, width), F32),
            shape((quarter, width), F32),
        ],
        [gelu, branch, low, middle, down],
        scratch=[pltpu.VMEM((n_tp, padded, width), F32)],
        cost=cost(700_000_000, 7_000_000),
    )

    def owned(sent, kept):
        cols = kept.shape[1]
        own, *outs = call(
            with_n(fold_body),
            "fold",
            [shape((part, cols), F32)] + [shape((part, cols))] * (n - 1),
            [kept, over_ctx(sent)],
        )
        got = [shift(x, k) for k, x in enumerate(outs, 1)]
        total, low = call(
            total_body, "total", [shape((part, cols), F32), shape((part, cols))], [own, *got]
        )
        return [total, over_ctx(low)]

    ffn_totals = owned(sent, kept)
    near = over_tp(near, 1)
    far = jnp.stack(
        [
            (keep[2] + near[1].astype(F32)).astype(LOW),
            (keep[3] + near[3].astype(F32)).astype(LOW),
        ]
    )
    far = over_tp(far, 2)
    layer_out, middle_grad, attn = call(
        rows_body,
        "rows",
        [shape((quarter, width)), shape((quarter, width), F32), shape((quarter, width))],
        [slot_counts, keep, near, far, own_middle, own_branch, vectors],
        scalars=1,
    )
    attns = spread_tp(attn)

    own_grads, other_grads, near, keep, own_act, sums = call(
        attend_back_body,
        "attend_back",
        [
            shape((slots, 3 * hw)),
            shape((slots, 2 * hw)),
            shape((4, padded, width)),
            shape((4, padded, width), F32),
            shape((quarter, width), F32),
            shape((8, width), F32),
        ],
        [back0, back1, back2, q, k, v, e, scales, turned, weights, act, other, sums],
        scratch=[pltpu.VMEM((n_tp, padded, width), F32)],
        cost=cost(4_000_000_000, 16_000_000),
    )
    near = over_tp(near, 1)
    sent, kept = call(
        head_grads_body,
        "head_grads",
        [shape((width, 2 * hw)), shape((width, 2 * hw), F32)],
        [own_grads, other_grads, normed_own, normed_other, mixed, *attns],
        scratch=[pltpu.VMEM((n_tp, quarter, hw), F32)],
        cost=cost(1_000_000_000, 6_000_000),
    )
    head_totals = owned(sent, kept)
    to_tp, to_ctx, to_far = call(
        halfway_body, "halfway", [shape((padded, width))] * 3, [keep, near]
    )
    from_tp = over_tp(to_tp, 2)
    from_ctx = over_ctx(to_ctx)
    pairs = [(i, i ^ (n_tp + 2)) for i in range(n_ctx * n_tp)]
    from_far = lax.ppermute(to_far, ("ctx", "tp"), pairs)
    (input_grad,) = call(
        input_body,
        "input",
        [shape((quarter, width))],
        [keep, near, from_tp, from_ctx, from_far, own_act, middle_grad, vectors],
    )
    up_grad, down_grad = call(
        ffn_finish_body, "ffn_finish", [shape((part, ff), F32), shape((part, ff), F32)], ffn_totals
    )
    qkv_grad, proj_grad = call(
        head_finish_body,
        "head_finish",
        [shape((3, part, hw), F32), shape((hw, part), F32)],
        head_totals,
    )

    shared = sums[:6]
    for bit in (1, 2):
        shared = shared + over_tp(shared, bit)
    sums = jnp.concatenate([shared, sums[6:]])
    sums = sums + over_ctx(sums)
    bit = 1
    while bit < n:
        sums = sums + lax.ppermute(sums, "shard", [(i, i ^ bit) for i in range(n)])
        bit *= 2
    vector_grads = lax.dynamic_slice_in_dim(sums[:6], lax.axis_index("shard") * part, part, 1)
    return (
        layer_out[None],
        input_grad[None],
        qkv_grad,
        proj_grad,
        up_grad,
        down_grad.T,
        vector_grads[:2],
        vector_grads[2:],
        sums[7, : 2 * hw].reshape(2, hw),
        sums[6],
    )


def solution(mesh):
    placed = (
        P("shard", "ctx", None),
        P("shard", None),
        P(None, "shard", "tp"),
        P("tp", "shard"),
        P("shard", "tp"),
        P("tp", "shard"),
        P(None, "shard"),
        P(None, "shard"),
        P(None, "tp"),
        P("tp"),
        P("shard", "ctx", None),
    )
    return jax.shard_map(
        per_device,
        mesh=mesh,
        in_specs=placed,
        out_specs=(
            P("shard", ("ctx", "tp"), None),
            P("shard", ("ctx", "tp"), None),
            P(None, "shard", "tp"),
            P("tp", "shard"),
            P("shard", "tp"),
            P("tp", "shard"),
            P(None, "shard"),
            P(None, "shard"),
            P(None, "tp"),
            P("tp"),
        ),
        check_vma=False,
    )
```

```python
import math

import jax
import jax.numpy as jnp
from jax import lax
from jax.experimental import pallas as pl
from jax.experimental.pallas import tpu as pltpu
from jax.sharding import PartitionSpec as P

HD = 64
EPS = 1e-06
NEG = -1e30
F32 = jnp.float32
LOW = jnp.bfloat16
VMEM = pl.BlockSpec(memory_space=pltpu.VMEM)
SMEM = pl.BlockSpec(memory_space=pltpu.SMEM)


def shape(dims, dtype=LOW):
    return jax.ShapeDtypeStruct(dims, dtype)


def call(body, name, out, args, scalars=0, scratch=(), cost=None, room=24):
    return pl.pallas_call(
        body,
        name=name,
        out_shape=out,
        in_specs=[SMEM] * scalars + [VMEM] * (len(args) - scalars),
        out_specs=[VMEM] * len(out),
        scratch_shapes=list(scratch),
        compiler_params=pltpu.CompilerParams(vmem_limit_bytes=room * 2**20),
        cost_estimate=cost,
    )(*args)


def cost(flops, moved, exps=0):
    return pl.CostEstimate(flops=flops, bytes_accessed=moved, transcendentals=exps)


def dot(left, right, left_dim=1, right_dim=0):
    return lax.dot_general(
        left, right, (((left_dim,), (right_dim,)), ((), ())), preferred_element_type=F32
    )


def norm_stats(values):
    centred = values - jnp.mean(values, axis=-1, keepdims=True)
    rate = lax.rsqrt(jnp.mean(centred * centred, axis=-1, keepdims=True) + EPS)
    return centred * rate, rate


def norm_back(grad, scaled, rate, gain):
    e = grad * gain
    inner = jnp.mean(e * scaled, axis=-1, keepdims=True)
    return rate * (e - jnp.mean(e, axis=-1, keepdims=True) - scaled * inner)


def own_other(counts):
    ctx = lax.axis_index("ctx")
    first, second = counts[0, 0], counts[0, 1]
    return jnp.where(ctx == 0, first, second), jnp.where(ctx == 0, second, first)


def wide(blocks):
    return jnp.concatenate(blocks, axis=1)


def to_chunks(value, ref):
    tp = lax.axis_index("tp")
    count = ref.shape[0]
    rows = value.shape[0] // count
    for g in range(count):
        ref[tp ^ g, :rows, :] = value[g * rows : (g + 1) * rows].astype(ref.dtype)


def folded_rows(rows):
    return (rows // 2 + 7) // 8 * 8


def fold_rows(value):
    top = folded_rows(value.shape[0])
    rest = value[top:]
    pad = jnp.zeros((top - rest.shape[0], value.shape[1]), value.dtype)
    if pad.shape[0]:
        rest = jnp.concatenate([rest, pad], axis=0)
    return wide([value[:top], rest])


def unfold_rows(value, rows):
    cols = value.shape[1] // 2
    return jnp.concatenate([value[:, :cols], value[: rows - value.shape[0], cols:]], axis=0)


def pack_body(qkv, gains, biases, proj, act, pack, pack_half, act_half):
    ctx = lax.axis_index("ctx")
    part, hw = qkv.shape[1], qkv.shape[2]
    width = pack.shape[1]
    pack[:part, :] = wide([qkv[0], qkv[1], qkv[2], proj[...].T])
    spare = pack.shape[0] - part
    vectors = jnp.concatenate(
        [gains[...].astype(F32), biases[...].astype(F32), jnp.zeros((spare - 6, part), F32)],
        axis=0,
    )
    pack[part:, :] = wide([vectors, jnp.zeros((spare, width - part), F32)]).astype(LOW)
    size = pack_half.shape[0]
    pack_half[...] = pack[pl.ds(pl.multiple_of(ctx * size, 16), size), :]
    size = act_half.shape[1]
    core = lax.axis_index("tp") % 2
    act_half[...] = act[:, pl.ds(pl.multiple_of(core * size, 128), size)]


def assemble(parts, held):
    n, rows, _ = held.shape
    shard, ctx = lax.axis_index("shard"), lax.axis_index("ctx")
    swapped = parts[-1]
    pairs = (n - 1) // 2
    held[shard] = parts[0][...]
    for k in range(1, pairs + 1):
        step = jnp.where(ctx == 0, n - k, k)
        held[(shard + step) % n] = parts[k][...]
        held[(shard + n - step) % n] = swapped[(k - 1) * rows : k * rows, :]
    far = (shard + n // 2) % n
    size = rows // 2
    held[far, pl.ds(pl.multiple_of(ctx * size, 8), size), :] = parts[-2][...]
    held[far, pl.ds(pl.multiple_of((1 - ctx) * size, 8), size), :] = swapped[pairs * rows :, :]


def split_sums(value):
    half = value.shape[1] // 2
    stacked = jnp.concatenate([value[:, :half], value[:, half:]], axis=0)
    high = stacked.astype(LOW)
    rest = (stacked - high.astype(F32)).astype(LOW)
    return jnp.concatenate([high, rest], axis=0)


def joined_sums(value):
    stacked = value[:16].astype(F32) + value[16:].astype(F32)
    return wide([stacked[:8], stacked[8:]])


def join_body(n, *refs):
    parts, (weights, proj, vectors, held) = refs[:-4], refs[-4:]
    assemble(parts, held)
    part = weights.shape[0] // n
    for g in range(n):
        weights[g * part : (g + 1) * part, :] = held[g, :part, :]
    vectors[...] = wide([held[g, part : part + 16, :part].astype(F32) for g in range(n)])[:8]
    cols = weights.shape[1] // 4
    half = weights.shape[0] // 2
    proj[...] = wide([weights[:half, 3 * cols :], weights[half:, 3 * cols :]])


def attend_body(
    counts, act, half_far, half_near, weights, vectors, biases, mixed_out, turned_out, scale_out,
    other, normed_own, normed_other, q_out, k_out, v_out, e_out,
):
    slots = act.shape[0]
    hw = biases.shape[1]
    core = lax.axis_index("tp") % 2
    size = half_far.shape[1]
    other[:, pl.ds(pl.multiple_of(core * size, 128), size)] = half_far[...]
    other[:, pl.ds(pl.multiple_of((1 - core) * size, 128), size)] = half_near[...]
    bias = biases[...].astype(F32)
    for src, dst in ((act, normed_own), (other, normed_other)):
        scaled, _ = norm_stats(src[...].astype(F32))
        dst[...] = (scaled * vectors[0:1] + vectors[2:3]).astype(LOW)
    queries = (dot(normed_own[...], weights[:, :hw]) + bias[0:1]).astype(LOW)
    q_out[...] = (queries.astype(F32) * (1.0 / math.sqrt(HD))).astype(LOW)
    for i, src in enumerate((normed_own, normed_other)):
        both = dot(src[...], weights[:, hw : 3 * hw])
        k_out[i] = both[:, :hw].astype(LOW)
        v_out[i] = (both[:, hw:] + bias[1:2]).astype(LOW)
    ids = lax.broadcasted_iota(jnp.int32, (slots, 1), 0)
    outs, scales = [], []
    for h in range(hw // HD):
        cols = slice(h * HD, (h + 1) * HD)
        query = q_out[:, cols]
        scores = [
            jnp.where(ids < count, dot(k_out[i][:, cols], query, 1, 1), NEG)
            for i, count in enumerate(own_other(counts))
        ]
        peak = jnp.maximum(*[jnp.max(s, axis=0, keepdims=True) for s in scores])
        mixed, total = 0.0, 0.0
        for i in range(2):
            e = jnp.exp(scores[i] - peak)
            total = total + jnp.sum(e, axis=0, keepdims=True)
            e_out[h, i] = e.astype(LOW)
            mixed = mixed + dot(v_out[i][:, cols], e_out[h, i], 0, 0)
        scales.append(1.0 / total)
        outs.append(mixed * scales[-1])
    turned = jnp.concatenate(outs, axis=0)
    turned_out[...] = turned
    mixed_out[...] = fold_rows(turned.T).astype(LOW)
    scales.append(jnp.zeros((8 - len(scales), slots), F32))
    scale_out[...] = jnp.concatenate(scales, axis=0).T


def hidden_body(n, *refs):
    (counts, act, *rest) = refs
    mixes, projs, rest = rest[:4], rest[4:8], rest[8:]
    vectors, hidden_bias, cot, *rest = rest
    ups, rest = rest[: n // 2 + 2], rest[n // 2 + 2 :]
    two_out, gelu_out, slope_out, branch_out, middle_out, up_out, proj, held = rest
    slots = act.shape[0]
    width = act.shape[1]
    own, _ = own_other(counts)
    valid = lax.broadcasted_iota(jnp.int32, (slots, 1), 0) < own
    branch_out[...] = jnp.where(valid, cot[...].astype(F32), 0.0).astype(LOW)
    top, bottom = 0.0, 0.0
    for j, (mixed, packed) in enumerate(zip(mixes, projs)):
        cols = packed.shape[1] // 2
        half = packed.shape[0]
        proj[j, :half, :] = packed[:, :cols]
        proj[j, half:, :] = packed[:, cols:]
        top = top + dot(mixed[:, :cols], proj[j], 1, 1)
        bottom = bottom + dot(mixed[:, cols:], proj[j], 1, 1)
    rows = slots - top.shape[0]
    middle = jnp.concatenate([top, bottom[:rows]], axis=0) + act[...].astype(F32) + vectors[4:5]
    middle_out[...] = middle
    scaled, _ = norm_stats(middle)
    two = (scaled * vectors[1:2] + vectors[3:4]).astype(LOW)
    two_out[...] = two
    assemble(ups, held)
    up = held[...].reshape(width, -1)
    up_out[...] = up
    hidden = dot(two, up) + hidden_bias[...].astype(F32)
    share = 0.5 * (1.0 + lax.erf(hidden * math.sqrt(0.5)))
    gelu_out[...] = (hidden * share).astype(LOW)
    bell = jnp.exp(hidden * hidden * -0.5) * (1.0 / math.sqrt(2.0 * math.pi))
    slope_out[...] = share + hidden * bell


def down_grads_body(n, branch, gelu, own, *rest):
    outs, total = rest[:-1], rest[-1]
    shard = lax.axis_index("shard")
    rows = own.shape[0]
    total[...] = dot(branch[...], gelu[...], 0, 0)
    own[...] = total[pl.ds(pl.multiple_of(shard * rows, 16), rows), :]
    for k, out in enumerate(outs, 1):
        at = (shard + k) % n * rows
        out[...] = total[pl.ds(pl.multiple_of(at, 16), rows), :].astype(LOW)


def middle_back_body(n, *refs):
    branch, slope, up, middle, vectors, proj, *rest = refs
    downs, rest = rest[: n // 2 + 2], rest[n // 2 + 2 :]
    back0, back1, back2, back3, hidden_out, low_out, down_out, sums, held = rest
    width = up.shape[0]
    assemble(downs, held)
    down = held[...].reshape(width, -1)
    down_out[...] = down
    branch_low = branch[...]
    grad_hidden = (dot(branch_low, down) * slope[...]).astype(LOW)
    hidden_out[...] = grad_hidden
    grad_two = dot(grad_hidden, up[...], 1, 1)
    scaled, rate = norm_stats(middle[...])
    back = norm_back(grad_two, scaled, rate, vectors[1:2])
    low = back.astype(LOW)
    low_out[...] = low
    back0[...] = fold_rows(dot(low, proj[0]) + dot(branch_low, proj[0]))
    for j, out in enumerate((back1, back2, back3), 1):
        out[...] = fold_rows(dot(low, proj[j])).astype(LOW)
    first_tp = jnp.where(lax.axis_index("tp") == 0, 1.0, 0.0)
    branch_sum = jnp.sum(branch_low.astype(F32), axis=0, keepdims=True) * first_tp
    sums[...] = jnp.concatenate(
        [
            jnp.sum(grad_two * scaled, axis=0, keepdims=True),
            jnp.sum(grad_two, axis=0, keepdims=True),
            branch_sum + jnp.sum(back, axis=0, keepdims=True),
            branch_sum,
            jnp.sum(grad_hidden.astype(F32), axis=0, keepdims=True),
            jnp.zeros((3, sums.shape[1]), F32),
        ],
        axis=0,
    )


def up_grads_body(two, hidden, low, branch, mix0, mix1, mix2, mix3, sent, kept, near, keep):
    ctx = lax.axis_index("ctx")
    slots = two.shape[0]
    up_grad = dot(two[...], hidden[...], 0, 0)
    half = up_grad.shape[1] // 2

    @pl.when(ctx == 0)
    def _():
        kept[...] = up_grad[:, :half]
        sent[...] = up_grad[:, half:].astype(LOW)

    @pl.when(ctx == 1)
    def _():
        kept[...] = up_grad[:, half:]
        sent[...] = up_grad[:, :half].astype(LOW)

    first_tp = jnp.where(lax.axis_index("tp") == 0, 1.0, 0.0)
    attn = (low[...].astype(F32) + first_tp * branch[...].astype(F32)).astype(LOW)
    grads = [
        dot(attn, unfold_rows(mix[...].astype(F32), slots).astype(LOW), 0, 0)
        for mix in (mix0, mix1, mix2, mix3)
    ]
    near[...] = wide([grads[1], grads[3]]).astype(LOW)
    keep[...] = wide([grads[0], grads[2]])


def proj_half_body(keep, near, own, out):
    cols = own.shape[1]
    half = out.shape[0]
    total = keep[...] + near[...].astype(F32)
    own[...] = total[:, :cols]
    out[...] = wide([total[:half, cols:], total[half:, cols:]]).astype(LOW)


def ffn_rows_body(gelu, branch, low, middle, down, near, keep, own_middle, own_branch, chunks):
    rows = own_middle.shape[0]
    chunks[:, rows - 2 :, :] = jnp.zeros_like(chunks[:, rows - 2 :, :])
    to_chunks(dot(gelu[...], down[...], 1, 1), chunks)
    near[0] = chunks[1].astype(LOW)
    near[1] = chunks[3].astype(LOW)
    keep[0] = chunks[0]
    keep[2] = chunks[2]
    to_chunks(low[...].astype(F32), chunks)
    near[2] = chunks[1].astype(LOW)
    near[3] = chunks[3].astype(LOW)
    keep[1] = chunks[0]
    keep[3] = chunks[2]
    to_chunks(middle[...], chunks)
    own_middle[...] = chunks[0, :rows, :]
    to_chunks(branch[...].astype(F32), chunks)
    own_branch[...] = chunks[0, :rows, :]


def rows_half_body(keep, near, out):
    for i, j in ((0, 1), (1, 3)):
        out[i] = (keep[2 + i] + near[j].astype(F32)).astype(LOW)


def rows_body(counts, keep, near, far, own_middle, own_branch, vectors, layer_out, middle_grad):
    own, _ = own_other(counts)
    rows = layer_out.shape[0]
    ids = lax.broadcasted_iota(jnp.int32, (rows, 1), 0) + lax.axis_index("tp") * rows
    mlp = keep[0] + near[0].astype(F32) + far[0].astype(F32)
    value = own_middle[...] + mlp[:rows] + vectors[5:6]
    layer_out[...] = jnp.where(ids < own, value, 0.0).astype(LOW)
    back = keep[1] + near[2].astype(F32) + far[1].astype(F32)
    middle_grad[...] = own_branch[...] + back[:rows]


def attend_back_body(
    back0, back1, back2, q, k, v, e, scales, turned, weights, act, other, sums_in,
    own_out, other_out, near, keep, own_act, sums, chunks,
):
    slots, hw = q.shape
    grad_mixed = back0[...] + back1[...].astype(F32) + back2[...].astype(F32)
    grad_mixed = unfold_rows(grad_mixed, slots).astype(LOW).astype(F32)
    scaled_grads = [
        grad_mixed[:, h * HD : (h + 1) * HD] * scales[:, h : h + 1] for h in range(hw // HD)
    ]
    scaled_grad = wide(scaled_grads)
    inner = scaled_grad.T * turned[...]
    scaled_low = scaled_grad.astype(LOW)
    scale = 1.0 / math.sqrt(HD)
    gq, gk, gv = [], ([], []), ([], [])
    for h in range(hw // HD):
        cols = slice(h * HD, (h + 1) * HD)
        grad = scaled_low[:, cols]
        row = jnp.sum(inner[cols], axis=0, keepdims=True)
        gq_head = 0.0
        for i in range(2):
            gv[i].append(dot(e[h, i], grad))
            probs_grad = dot(v[i][:, cols], grad, 1, 1)
            scores_grad = (e[h, i].astype(F32) * (probs_grad - row)).astype(LOW)
            gk[i].append(dot(scores_grad, q[:, cols]))
            gq_head = gq_head + dot(k[i][:, cols], scores_grad, 0, 0)
        gq.append(gq_head * scale)
    gq = jnp.concatenate(gq, axis=0).T
    own_out[...] = wide([gq, *gk[0], *gv[0]]).astype(LOW)
    other_out[...] = wide([*gk[1], *gv[1]]).astype(LOW)
    rows = own_act.shape[0]
    chunks[:, rows - 2 :, :] = jnp.zeros_like(chunks[:, rows - 2 :, :])
    gain_sum, shift_sum = 0.0, 0.0
    for i, src in enumerate((act, other)):
        if i == 0:
            grad = dot(own_out[...], weights[:, : 3 * hw], 1, 1)
        else:
            grad = dot(other_out[...], weights[:, hw : 3 * hw], 1, 1)
        scaled, _ = norm_stats(src[...].astype(F32))
        gain_sum = gain_sum + jnp.sum(grad * scaled, axis=0, keepdims=True)
        shift_sum = shift_sum + jnp.sum(grad, axis=0, keepdims=True)
        to_chunks(grad, chunks)
        near[2 * i] = chunks[1].astype(LOW)
        near[2 * i + 1] = chunks[3].astype(LOW)
        keep[2 * i] = chunks[0]
        keep[2 * i + 1] = chunks[2]
    to_chunks(act[...].astype(F32), chunks)
    own_act[...] = chunks[0, :rows, :]
    ones = jnp.ones((8, slots), LOW)
    own_sums = dot(ones, own_out[...])[0:1]
    other_sums = dot(ones, other_out[...])[0:1]
    head_v = own_sums[:, 2 * hw :] + other_sums[:, hw:]
    pad = jnp.zeros((1, sums.shape[1] - 2 * hw), F32)
    sums[...] = jnp.concatenate(
        [
            gain_sum,
            sums_in[0:1],
            shift_sum,
            sums_in[1:2],
            sums_in[2:3],
            sums_in[3:4],
            sums_in[4:5],
            wide([own_sums[:, :hw], head_v, pad]),
        ],
        axis=0,
    )


def head_grads_body(
    own, other, normed_own, normed_other, proj_own, proj_far, sums, sent, kept
):
    ctx = lax.axis_index("ctx")
    hw = own.shape[1] // 3
    rows = kept.shape[0]
    far = jnp.concatenate([proj_far[:, :hw], proj_far[:, hw:]], axis=0)
    proj_grad = proj_own[...] + far.astype(F32)
    from_own = dot(normed_own[...], own[...], 0, 0)
    from_other = dot(normed_other[...], other[...], 0, 0)
    k_grad = from_own[:, hw : 2 * hw] + from_other[:, :hw]
    v_grad = from_own[:, 2 * hw :] + from_other[:, hw:]
    early = wide([from_own[:, :hw], k_grad])
    late = wide([v_grad, proj_grad])
    sent[rows:, :] = split_sums(sums[...])

    @pl.when(ctx == 0)
    def _():
        kept[...] = early
        sent[:rows, :] = late.astype(LOW)

    @pl.when(ctx == 1)
    def _():
        kept[...] = late
        sent[:rows, :] = early.astype(LOW)


def fold_body(n, kept, got, own, *outs):
    shard = lax.axis_index("shard")
    rows = own.shape[0]

    def summed(owner):
        at = pl.ds(pl.multiple_of(owner * rows, 16), rows)
        return kept[at, :] + got[at, :].astype(F32)

    own[...] = summed(shard)
    for k, out in enumerate(outs, 1):
        out[...] = summed((shard + k) % n).astype(LOW)


def head_fold_body(n, kept, got, sums, own, own_sums, *outs):
    shard = lax.axis_index("shard")
    rows = own.shape[0]
    total = sums[...] + joined_sums(got[n * rows :, :])
    own_sums[...] = total
    packed = split_sums(total)

    def summed(owner):
        at = pl.ds(pl.multiple_of(owner * rows, 16), rows)
        return kept[at, :] + got[at, :].astype(F32)

    own[...] = summed(shard)
    for k, out in enumerate(outs, 1):
        out[:rows, :] = summed((shard + k) % n).astype(LOW)
        out[rows:, :] = packed


def total_body(own, *refs):
    got, total, low = refs[:-2], refs[-2], refs[-1]
    value = own[...]
    for ref in got:
        value = value + ref[...].astype(F32)
    total[...] = value
    low[...] = value.astype(LOW)


def head_total_body(own, sums, *refs):
    got, (total, low, total_sums) = refs[:-3], refs[-3:]
    rows = own.shape[0]
    value = own[...]
    vectors = sums[...]
    for ref in got:
        value = value + ref[:rows, :].astype(F32)
        vectors = vectors + joined_sums(ref[rows:, :])
    total[...] = value
    low[...] = value.astype(LOW)
    total_sums[...] = vectors


def ffn_finish_body(down_mine, down_other, up_mine, up_other, up_grad, down_grad):
    first = lax.axis_index("ctx") == 0
    half = up_mine.shape[1]
    theirs = up_other[...].astype(F32)
    mine = up_mine[...]
    up_grad[:, :half] = jnp.where(first, mine, theirs)
    up_grad[:, half:] = jnp.where(first, theirs, mine)
    down_grad[...] = down_mine[...] + down_other[...].astype(F32)


def finish_body(
    n, mine, other, sums_near, sums_far, qkv_grad, proj_grad, gains, biases, heads, hidden
):
    first = lax.axis_index("ctx") == 0
    shard = lax.axis_index("shard")
    theirs = other[...].astype(F32)
    early = jnp.where(first, mine[...], theirs)
    late = jnp.where(first, theirs, mine[...])
    hw = early.shape[1] // 2
    qkv_grad[0] = early[:, :hw]
    qkv_grad[1] = early[:, hw:]
    qkv_grad[2] = late[:, :hw]
    proj_grad[...] = late[:, hw:].T
    shared = sums_near[...] + sums_far[...]
    part = gains.shape[1]
    own = 0.0
    for g in range(n):
        own = own + jnp.where(shard == g, shared[:, g * part : (g + 1) * part], 0.0)
    gains[...] = own[0:2]
    biases[...] = own[2:6]


def input_half_body(keep, near, own, out):
    own[0] = keep[0] + near[0].astype(F32)
    own[1] = keep[2] + near[2].astype(F32)
    out[0] = (keep[1] + near[1].astype(F32)).astype(LOW)
    out[1] = (keep[3] + near[3].astype(F32)).astype(LOW)


def input_cross_body(own, far, kept, out):
    kept[...] = own[0] + far[0].astype(F32)
    out[...] = (own[1] + far[1].astype(F32)).astype(LOW)


def input_body(kept, cross, own_act, middle_grad, vectors, out):
    rows = out.shape[0]
    grad = kept[...] + cross[...].astype(F32)
    scaled, rate = norm_stats(own_act[...])
    back = norm_back(grad[:rows], scaled, rate, vectors[0:1])
    out[...] = (middle_grad[...] + back).astype(LOW)


def per_device(
    activations,
    slot_counts,
    qkv_weight,
    proj_weight,
    up_weight,
    down_weight,
    norm_gains,
    row_biases,
    head_biases,
    hidden_bias,
    cotangent,
):
    images, slots, width = activations.shape
    n = lax.axis_size("shard")
    n_ctx = lax.axis_size("ctx")
    n_tp = lax.axis_size("tp")
    assert images == 1 and n_ctx == 2 and n_tp == 4 and n % 2 == 0
    part = width // n
    hw = qkv_weight.shape[2]
    ff = up_weight.shape[1]
    quarter = slots // n_tp
    padded = (quarter + 7) // 8 * 8
    fold = folded_rows(slots)
    heads = hw // HD
    ctx = lax.axis_index("ctx")

    def over_ctx(x):
        return lax.ppermute(x, "ctx", [(i, i ^ 1) for i in range(n_ctx)])

    def over_tp(x, bit):
        return lax.ppermute(x, "tp", [(i, i ^ bit) for i in range(n_tp)])

    def shift(x, k):
        return lax.ppermute(x, "shard", [(i, (i + k) % n) for i in range(n)])

    def shift_by_ctx(x, k):
        moves = [
            (i * n_ctx + r, ((i + (k if r == 0 else n - k)) % n) * n_ctx + r)
            for i in range(n)
            for r in range(n_ctx)
        ]
        return lax.ppermute(x, ("shard", "ctx"), moves)

    def fetch(pack, pack_half):
        mine = [shift_by_ctx(pack, k) for k in range(1, (n - 1) // 2 + 1)]
        mine.append(shift(pack_half, n // 2))
        return [pack] + mine + [over_ctx(jnp.concatenate(mine, axis=0))]

    def with_n(body):
        def run(*refs):
            body(n, *refs)

        return run

    def spread_tp(x):
        far = over_tp(x, 2)
        return [x, over_tp(x, 1), far, over_tp(far, 1)]

    def row_half(x):
        size = x.shape[0] // 2
        return lax.dynamic_slice_in_dim(x, ctx * size, size, 0)

    def after(x, *others):
        return lax.optimization_barrier((x, *others))[0]

    act = activations[0]
    rows = -(-(part + 6) // 32) * 32
    pack, pack_half, act_half = call(
        pack_body,
        "pack",
        [shape((rows, width)), shape((rows // 2, width)), shape((slots, width // 2))],
        [qkv_weight, norm_gains, row_biases, proj_weight, act],
        room=58,
    )
    half_far = over_ctx(act_half)
    half_near = over_tp(half_far, 1)
    pack_parts = fetch(pack, pack_half)
    up_late = after(up_weight, half_far)
    up_parts = fetch(up_late, row_half(up_late))
    down_late = after(down_weight.T, up_parts[1])
    down_parts = fetch(down_late, row_half(down_late))

    weights, proj, vectors = call(
        with_n(join_body),
        "join",
        [shape((width, width)), shape((width // 2, 2 * hw)), shape((8, width), F32)],
        pack_parts,
        scratch=[pltpu.VMEM((n, rows, width), LOW)],
    )
    (mixed, turned, scales, other, normed_own, normed_other, q, k, v, e) = call(
        attend_body,
        "attend",
        [
            shape((fold, 2 * hw)),
            shape((hw, slots), F32),
            shape((slots, 8), F32),
            shape((slots, width)),
            shape((slots, width)),
            shape((slots, width)),
            shape((slots, hw)),
            shape((2, slots, hw)),
            shape((2, slots, hw)),
            shape((heads, 2, slots, slots)),
        ],
        [slot_counts, act, half_far, half_near, weights, vectors, head_biases],
        scalars=1,
        cost=cost(3_000_000_000, 12_000_000, 2_000_000),
    )
    projs = spread_tp(proj)
    mixes = spread_tp(mixed)
    two, gelu, slope, branch, middle, up, proj_full = call(
        with_n(hidden_body),
        "hidden",
        [
            shape((slots, width)),
            shape((slots, ff)),
            shape((slots, ff), F32),
            shape((slots, width)),
            shape((slots, width), F32),
            shape((width, ff)),
            shape((n_tp, width, hw)),
        ],
        [slot_counts, act, *mixes, *projs, vectors, hidden_bias.reshape(1, ff), cotangent[0]]
        + up_parts,
        scalars=1,
        scratch=[pltpu.VMEM((n, part, ff), LOW)],
        cost=cost(1_500_000_000, 8_000_000, 1_000_000),
    )
    own, *outs = call(
        with_n(down_grads_body),
        "down_grads",
        [shape((part, ff), F32)] + [shape((part, ff))] * (n - 1),
        [branch, gelu],
        scratch=[pltpu.VMEM((width, ff), F32)],
        cost=cost(600_000_000, 3_000_000),
    )
    got = [shift(x, k) for k, x in enumerate(outs, 1)]
    down_mine, low = call(
        total_body, "down_total", [shape((part, ff), F32), shape((part, ff))], [own, *got]
    )
    down_other = over_ctx(low)
    back0, back1, back2, back3, hidden, low, down, sums = call(
        with_n(middle_back_body),
        "middle_back",
        [shape((fold, 2 * hw), F32)]
        + [shape((fold, 2 * hw))] * 3
        + [shape((slots, ff)), shape((slots, width)), shape((width, ff)), shape((8, width), F32)],
        [branch, slope, up, middle, vectors, proj_full] + down_parts,
        scratch=[pltpu.VMEM((n, part, ff), LOW)],
        cost=cost(2_000_000_000, 8_000_000),
    )
    back1 = over_tp(back1, 1)
    back2 = (back2.astype(F32) + over_tp(back3, 1).astype(F32)).astype(LOW)
    back2 = over_tp(back2, 2)
    sent, kept, proj_near, proj_keep = call(
        up_grads_body,
        "up_grads",
        [
            shape((width, ff // 2)),
            shape((width, ff // 2), F32),
            shape((width, 2 * hw)),
            shape((width, 2 * hw), F32),
        ],
        [two, hidden, low, branch, *mixes],
        cost=cost(1_300_000_000, 7_000_000),
    )
    up_got = over_ctx(sent)
    proj_near = over_tp(proj_near, 1)
    near, keep, own_middle, own_branch = call(
        ffn_rows_body,
        "ffn_rows",
        [
            shape((4, padded, width)),
            shape((4, padded, width), F32),
            shape((quarter, width), F32),
            shape((quarter, width), F32),
        ],
        [gelu, branch, low, middle, down],
        scratch=[pltpu.VMEM((n_tp, padded, width), F32)],
        cost=cost(700_000_000, 7_000_000),
    )
    proj_own, proj_far = call(
        proj_half_body,
        "proj_half",
        [shape((width, hw), F32), shape((width // 2, 2 * hw))],
        [proj_keep, proj_near],
    )
    proj_far = over_tp(after(proj_far, back2), 2)
    near = over_tp(after(near, back2), 1)
    (far,) = call(rows_half_body, "rows_half", [shape((2, padded, width))], [keep, near])
    far = over_tp(far, 2)
    layer_out, middle_grad = call(
        rows_body,
        "rows",
        [shape((quarter, width)), shape((quarter, width), F32)],
        [slot_counts, keep, near, far, own_middle, own_branch, vectors],
        scalars=1,
    )
    up_own, *outs = call(
        with_n(fold_body),
        "up_fold",
        [shape((part, ff // 2), F32)] + [shape((part, ff // 2))] * (n - 1),
        [kept, up_got],
    )
    got = [shift(x, k) for k, x in enumerate(outs, 1)]
    up_mine, low = call(
        total_body, "up_total", [shape((part, ff // 2), F32), shape((part, ff // 2))], [up_own, *got]
    )
    up_other = over_ctx(low)

    own_grads, other_grads, near, keep, own_act, sums = call(
        attend_back_body,
        "attend_back",
        [
            shape((slots, 3 * hw)),
            shape((slots, 2 * hw)),
            shape((4, padded, width)),
            shape((4, padded, width), F32),
            shape((quarter, width), F32),
            shape((8, width), F32),
        ],
        [back0, back1, back2, q, k, v, e, scales, turned, weights, act, other, sums],
        scratch=[pltpu.VMEM((n_tp, padded, width), F32)],
        cost=cost(4_000_000_000, 16_000_000),
    )
    sent, kept = call(
        head_grads_body,
        "head_grads",
        [shape((width + 32, 2 * hw)), shape((width, 2 * hw), F32)],
        [own_grads, other_grads, normed_own, normed_other, proj_own, proj_far, sums],
        cost=cost(1_000_000_000, 6_000_000),
    )
    head_own, head_sums, *outs = call(
        with_n(head_fold_body),
        "head_fold",
        [shape((part, 2 * hw), F32), shape((8, width), F32)]
        + [shape((part + 32, 2 * hw))] * (n - 1),
        [kept, over_ctx(sent), sums],
    )
    got = [shift(x, k) for k, x in enumerate(outs, 1)]
    head_mine, low, head_sums = call(
        head_total_body,
        "head_total",
        [shape((part, 2 * hw), F32), shape((part, 2 * hw)), shape((8, width), F32)],
        [head_own, head_sums, *got],
    )
    head_other = over_ctx(low)
    sums_near = head_sums + over_tp(head_sums, 1)
    sums_far = over_tp(sums_near, 2)

    near = over_tp(near, 1)
    own, far = call(
        input_half_body,
        "input_half",
        [shape((2, padded, width), F32), shape((2, padded, width))],
        [keep, near],
    )
    kept, cross = call(
        input_cross_body,
        "input_cross",
        [shape((padded, width), F32), shape((padded, width))],
        [own, over_tp(far, 2)],
    )
    (input_grad,) = call(
        input_body,
        "input",
        [shape((quarter, width))],
        [kept, over_ctx(cross), own_act, middle_grad, vectors],
    )
    up_grad, down_grad = call(
        ffn_finish_body,
        "ffn_finish",
        [shape((part, ff), F32), shape((part, ff), F32)],
        [down_mine, down_other, up_mine, up_other],
    )
    qkv_grad, proj_grad, gains_grad, biases_grad = call(
        with_n(lambda n, *refs: finish_body(n, *refs, None, None)),
        "finish",
        [
            shape((3, part, hw), F32),
            shape((hw, part), F32),
            shape((2, part), F32),
            shape((4, part), F32),
        ],
        [head_mine, head_other, sums_near, sums_far],
    )
    return (
        layer_out[None],
        input_grad[None],
        qkv_grad,
        proj_grad,
        up_grad,
        down_grad.T,
        gains_grad,
        biases_grad,
        head_sums[7, : 2 * hw].reshape(2, hw),
        head_sums[6],
    )


def solution(mesh):
    placed = (
        P("shard", "ctx", None),
        P("shard", None),
        P(None, "shard", "tp"),
        P("tp", "shard"),
        P("shard", "tp"),
        P("tp", "shard"),
        P(None, "shard"),
        P(None, "shard"),
        P(None, "tp"),
        P("tp"),
        P("shard", "ctx", None),
    )
    return jax.shard_map(
        per_device,
        mesh=mesh,
        in_specs=placed,
        out_specs=(
            P("shard", ("ctx", "tp"), None),
            P("shard", ("ctx", "tp"), None),
            P(None, "shard", "tp"),
            P("tp", "shard"),
            P("shard", "tp"),
            P("tp", "shard"),
            P(None, "shard"),
            P(None, "shard"),
            P(None, "tp"),
            P("tp"),
        ),
        check_vma=False,
    )
```

```python
import functools
import math

import jax
import jax.numpy as jnp
from jax import lax
from jax.experimental import pallas as pl
from jax.experimental.pallas import tpu as pltpu
from jax.sharding import PartitionSpec as P

HD = 64
EPS = 1e-06
NEG = -1e30
F32 = jnp.float32
LOW = jnp.bfloat16
VMEM = pl.BlockSpec(memory_space=pltpu.VMEM)
SMEM = pl.BlockSpec(memory_space=pltpu.SMEM)


def shape(dims, dtype=LOW):
    return jax.ShapeDtypeStruct(dims, dtype)


def call(body, name, out, args, scalars, scratch, room, token, weight):
    count = len(args)

    def kernel(*refs):
        body(*refs[:count], *refs[count + (token is not None) :])

    specs = [SMEM] * scalars + [VMEM] * (count - scalars)
    if token is not None:
        specs.append(pl.BlockSpec(memory_space=pl.ANY))
        args = [*args, token]
    return pl.pallas_call(
        kernel,
        name=name,
        out_shape=out,
        in_specs=specs,
        out_specs=[VMEM] * len(out),
        scratch_shapes=list(scratch),
        compiler_params=pltpu.CompilerParams(vmem_limit_bytes=room * 2**20),
        cost_estimate=pl.CostEstimate(
            flops=weight * 10**9 + 1, bytes_accessed=weight * 10**6 + 1, transcendentals=0
        ),
    )(*args)


def dot(left, right, left_dim=1, right_dim=0):
    return lax.dot_general(
        left, right, (((left_dim,), (right_dim,)), ((), ())), preferred_element_type=F32
    )


def norm_stats(values):
    centred = values - jnp.mean(values, axis=-1, keepdims=True)
    rate = lax.rsqrt(jnp.mean(centred * centred, axis=-1, keepdims=True) + EPS)
    return centred * rate, rate


def norm_back(grad, scaled, rate, gain):
    e = grad * gain
    inner = jnp.mean(e * scaled, axis=-1, keepdims=True)
    return rate * (e - jnp.mean(e, axis=-1, keepdims=True) - scaled * inner)


def own_other(counts):
    ctx = lax.axis_index("ctx")
    first, second = counts[0, 0], counts[0, 1]
    return jnp.where(ctx == 0, first, second), jnp.where(ctx == 0, second, first)


def wide(blocks):
    return jnp.concatenate(blocks, axis=1)


def to_chunks(value, ref):
    tp = lax.axis_index("tp")
    count = ref.shape[0]
    rows = value.shape[0] // count
    for g in range(count):
        ref[tp ^ g, :rows, :] = value[g * rows : (g + 1) * rows].astype(ref.dtype)


def folded_rows(rows):
    return (rows // 2 + 7) // 8 * 8


def fold_rows(value):
    top = folded_rows(value.shape[0])
    rest = value[top:]
    pad = jnp.zeros((top - rest.shape[0], value.shape[1]), value.dtype)
    if pad.shape[0]:
        rest = jnp.concatenate([rest, pad], axis=0)
    return wide([value[:top], rest])


def unfold_rows(value, rows):
    cols = value.shape[1] // 2
    return jnp.concatenate([value[:, :cols], value[: rows - value.shape[0], cols:]], axis=0)


def pack_body(qkv, gains, biases, proj, act, pack, pack_half, act_half):
    part, hw = qkv.shape[1], qkv.shape[2]
    width = pack.shape[1]
    pack[:part, :] = wide([qkv[0], qkv[1], qkv[2], proj[...].T])
    spare = pack.shape[0] - part
    vectors = jnp.concatenate(
        [gains[...].astype(F32), biases[...].astype(F32), jnp.zeros((spare - 6, part), F32)],
        axis=0,
    )
    pack[part:, :] = wide([vectors, jnp.zeros((spare, width - part), F32)]).astype(LOW)
    size = pack_half.shape[0]
    at = pl.multiple_of(lax.axis_index("ctx") * size, 16)
    pack_half[...] = pack[pl.ds(at, size), :]
    size = act_half.shape[1]
    core = lax.axis_index("tp") % 2
    act_half[...] = act[:, pl.ds(pl.multiple_of(core * size, 128), size)]


def assemble(parts, held):
    n, rows, _ = held.shape
    shard, ctx = lax.axis_index("shard"), lax.axis_index("ctx")
    pairs = (n - 1) // 2
    held[shard] = parts[0][...]
    for k in range(1, pairs + 1):
        step = jnp.where(ctx == 0, n - k, k)
        held[(shard + step) % n] = parts[2 * k - 1][...]
        held[(shard + n - step) % n] = parts[2 * k][...]
    far = (shard + n // 2) % n
    size = rows // 2
    held[far, pl.ds(pl.multiple_of(ctx * size, 8), size), :] = parts[-2][...]
    held[far, pl.ds(pl.multiple_of((1 - ctx) * size, 8), size), :] = parts[-1][...]


def mark_body(value, out):
    out[...] = value[:8, :128].astype(F32)


def half_body(block, out):
    size = out.shape[0]
    at = pl.multiple_of(lax.axis_index("ctx") * size, 8)
    out[...] = block[pl.ds(at, size), :]


def add_body(kept, proj_kept, near, total, proj_total, out, proj_out):
    rows = out.shape[0]
    total[...] = kept[0] + near[:rows, :].astype(F32)
    out[...] = (kept[1] + near[rows : 2 * rows, :].astype(F32)).astype(LOW)
    both = proj_kept[...] + near[2 * rows :, :].astype(F32)
    cols = both.shape[1] // 2
    half = proj_out.shape[0]
    proj_total[...] = both[:, :cols]
    proj_out[...] = wide([both[:half, cols:], both[half:, cols:]]).astype(LOW)


def pair_body(*refs):
    row = 0
    for ref in refs[:-1]:
        refs[-1][row : row + ref.shape[0], :] = ref[...]
        row += ref.shape[0]


def split_sums(value):
    high = value.astype(LOW).astype(F32)
    return jnp.concatenate([high, value - high], axis=0).astype(LOW)


def joined_sums(value):
    wide_value = value.astype(F32)
    return wide_value[:8] + wide_value[8:]


def join_body(n, *refs):
    half_far, half_near, *parts = refs[:-5]
    weights, proj, vectors, other, held = refs[-5:]
    core = lax.axis_index("tp") % 2
    size = half_far.shape[1]
    other[:, pl.ds(pl.multiple_of(core * size, 128), size)] = half_far[...]
    other[:, pl.ds(pl.multiple_of((1 - core) * size, 128), size)] = half_near[...]
    assemble(parts, held)
    part = weights.shape[0] // n
    for g in range(n):
        weights[g * part : (g + 1) * part, :] = held[g, :part, :]
    vectors[...] = wide([held[g, part : part + 16, :part].astype(F32) for g in range(n)])[:8]
    cols = weights.shape[1] // 4
    half = weights.shape[0] // 2
    proj[...] = wide([weights[:half, 3 * cols :], weights[half:, 3 * cols :]])


def attend_body(
    counts, act, other, weights, vectors, biases, mixed_out, turned_out, scale_out,
    normed_own, normed_other, q_out, k_out, v_out, e_out,
):
    slots = act.shape[0]
    hw = biases.shape[1]
    bias = biases[...].astype(F32)
    for src, dst in ((act, normed_own), (other, normed_other)):
        scaled, _ = norm_stats(src[...].astype(F32))
        dst[...] = (scaled * vectors[0:1] + vectors[2:3]).astype(LOW)
    queries = (dot(normed_own[...], weights[:, :hw]) + bias[0:1]).astype(LOW)
    q_out[...] = (queries.astype(F32) * (1.0 / math.sqrt(HD))).astype(LOW)
    for i, src in enumerate((normed_own, normed_other)):
        both = dot(src[...], weights[:, hw : 3 * hw])
        k_out[i] = both[:, :hw].astype(LOW)
        v_out[i] = (both[:, hw:] + bias[1:2]).astype(LOW)
    ids = lax.broadcasted_iota(jnp.int32, (slots, 1), 0)
    outs, scales = [], []
    for h in range(hw // HD):
        cols = slice(h * HD, (h + 1) * HD)
        query = q_out[:, cols]
        scores = [
            jnp.where(ids < count, dot(k_out[i][:, cols], query, 1, 1), NEG)
            for i, count in enumerate(own_other(counts))
        ]
        peak = jnp.maximum(*[jnp.max(s, axis=0, keepdims=True) for s in scores])
        mixed, total = 0.0, 0.0
        for i in range(2):
            e = jnp.exp(scores[i] - peak)
            total = total + jnp.sum(e, axis=0, keepdims=True)
            e_out[h, i] = e.astype(LOW)
            mixed = mixed + dot(v_out[i][:, cols], e_out[h, i], 0, 0)
        scales.append(1.0 / total)
        outs.append(mixed * scales[-1])
    turned = jnp.concatenate(outs, axis=0)
    turned_out[...] = turned
    mixed_out[...] = fold_rows(turned.T).astype(LOW)
    scales.append(jnp.zeros((8 - len(scales), slots), F32))
    scale_out[...] = jnp.concatenate(scales, axis=0).T


def unpair(mixed, mixed_far, proj, proj_far, paired):
    rows, more = mixed.shape[0], proj.shape[0]
    cuts = [0, rows, 2 * rows, 2 * rows + more, 2 * (rows + more)]
    near, cross, proj_near, proj_cross = [paired[a:b, :] for a, b in zip(cuts, cuts[1:])]
    return (
        (mixed[...], near, mixed_far[...], cross),
        (proj[...], proj_near, proj_far[...], proj_cross),
    )


def hidden_body(n, *refs):
    (counts, act, *rest) = refs
    mixed, mixed_far, packed, packed_far, paired, vectors, hidden_bias, cot, *rest = rest
    mixes, projs = unpair(mixed, mixed_far, packed, packed_far, paired)
    ups, rest = rest[: n + 1], rest[n + 1 :]
    two_out, gelu_out, slope_out, branch_out, middle_out, up_out, proj, held = rest
    slots = act.shape[0]
    width = act.shape[1]
    own, _ = own_other(counts)
    valid = lax.broadcasted_iota(jnp.int32, (slots, 1), 0) < own
    branch_out[...] = jnp.where(valid, cot[...].astype(F32), 0.0).astype(LOW)
    top, bottom = 0.0, 0.0
    for j, (mixed, packed) in enumerate(zip(mixes, projs)):
        cols = packed.shape[1] // 2
        half = packed.shape[0]
        proj[j, :half, :] = packed[:, :cols]
        proj[j, half:, :] = packed[:, cols:]
        top = top + dot(mixed[:, :cols], proj[j], 1, 1)
        bottom = bottom + dot(mixed[:, cols:], proj[j], 1, 1)
    rows = slots - top.shape[0]
    middle = jnp.concatenate([top, bottom[:rows]], axis=0) + act[...].astype(F32) + vectors[4:5]
    middle_out[...] = middle
    scaled, _ = norm_stats(middle)
    two = (scaled * vectors[1:2] + vectors[3:4]).astype(LOW)
    two_out[...] = two
    assemble(ups, held)
    up = held[...].reshape(width, -1)
    up_out[...] = up
    hidden = dot(two, up) + hidden_bias[...].astype(F32)
    share = 0.5 * (1.0 + lax.erf(hidden * math.sqrt(0.5)))
    gelu_out[...] = (hidden * share).astype(LOW)
    bell = jnp.exp(hidden * hidden * -0.5) * (1.0 / math.sqrt(2.0 * math.pi))
    slope_out[...] = share + hidden * bell


def block(ref, owner, rows):
    return ref[pl.ds(pl.multiple_of(owner * rows, 8), rows), :]


def down_grads_body(n, branch, gelu, total, up_half, down_half):
    rows = total.shape[0] // n
    half = up_half.shape[0]
    total[...] = dot(branch[...], gelu[...], 0, 0)
    far = (lax.axis_index("shard") + n // 2) % n
    up_half[...] = block(total, 2 * far, half).astype(LOW)
    down_half[...] = block(total, 2 * far + 1, half).astype(LOW)


def both_ways_body(n, left, total, got_up, got_down, up_out, down_out):
    shard = lax.axis_index("shard")
    rows = total.shape[0] // n
    for owner, got, out, last in (
        ((shard + left) % n, got_up, up_out, 0),
        ((shard + n - left) % n, got_down, down_out, 1),
    ):
        value = block(total, owner, rows)
        half = got.shape[0]
        if half == rows:
            out[...] = (value + got[...].astype(F32)).astype(LOW)
        else:
            both = [value[:half], value[half:]]
            both[last] = both[last] + got[...].astype(F32)
            out[...] = jnp.concatenate(both, axis=0).astype(LOW)


def both_ways_end_body(n, total, got_up, got_down, own, low):
    rows = own.shape[0]
    value = block(total, lax.axis_index("shard"), rows)
    value = value + got_up[...].astype(F32) + got_down[...].astype(F32)
    own[...] = value
    low[...] = value.astype(LOW)


def give(n, value, sent):
    shard, ctx = lax.axis_index("shard"), lax.axis_index("ctx")
    rows = value.shape[0] // n
    half = rows // 2
    theirs = jnp.where(ctx == 0, n - 1, 1)
    far = n // 2
    for k in range(1, far):
        owner = (shard + theirs * k) % n
        sent[(k - 1) * rows : k * rows, :] = block(value, owner, rows).astype(LOW)
    at = (far - 1) * rows
    for i, owner in enumerate(((shard + far) % n, shard)):
        piece = block(value, 2 * owner + (1 - ctx), half)
        sent[at + i * half : at + (i + 1) * half, :] = piece.astype(LOW)


def ring_first_body(n, value, got, out):
    shard, ctx = lax.axis_index("shard"), lax.axis_index("ctx")
    rows = value.shape[0] // n
    half = rows // 2
    at = (n // 2 - 1) * rows
    far = (shard + n // 2) % n
    piece = block(value, 2 * far + ctx, half) + got[at : at + half, :].astype(F32)
    out[...] = piece.astype(LOW)


def add_half(value, piece):
    ctx = lax.axis_index("ctx")
    zeros = jnp.zeros_like(piece)
    low = jnp.where(ctx == 0, piece, zeros)
    high = jnp.where(ctx == 0, zeros, piece)
    return value + jnp.concatenate([low, high], axis=0)


def ring_step_body(n, left, sums_too, value, got, came, *refs):
    shard, ctx = lax.axis_index("shard"), lax.axis_index("ctx")
    rows = value.shape[0] // n
    out = refs[-1]
    owner = (shard + jnp.where(ctx == 0, left, n - left)) % n
    first = left == n // 2 - 1
    piece = came[: rows // 2 if first else rows, :].astype(F32)
    total = block(value, owner, rows) + got[(left - 1) * rows : left * rows, :].astype(F32)
    total = add_half(total, piece) if first else total + piece
    out[:rows, :] = total.astype(LOW)
    if sums_too:
        more = joined_sums(came[piece.shape[0] :, :])
        if first:
            more = jnp.where(ctx == 0, more, 0.0)
        out[rows:, :] = split_sums(refs[0][...] + more)


def ring_end_body(n, sums_too, value, got, came, *refs):
    shard, ctx = lax.axis_index("shard"), lax.axis_index("ctx")
    rows = value.shape[0] // n
    half = rows // 2
    at = (n // 2 - 1) * rows + half
    piece = block(value, 2 * shard + ctx, half) + got[at : at + half, :].astype(F32)
    total = add_half(came[:rows, :].astype(F32), piece)
    if sums_too:
        both, own, low, sums = refs
        value_sums = jnp.where(ctx == 0, both[...], 0.0) + joined_sums(came[rows:, :])
        sums[...] = value_sums
        low[rows:, :] = split_sums(value_sums)
    else:
        own, low = refs
    own[...] = total
    low[:rows, :] = total.astype(LOW)


def middle_back_body(n, *refs):
    branch, slope, up, middle, vectors, proj, mixed, mixed_far, paired, *rest = refs
    downs, rest = rest[: n + 1], rest[n + 1 :]
    near, keep, proj_keep, hidden_out, low_out, down_out, sums, held = rest
    width = up.shape[0]
    assemble(downs, held)
    down = held[...].reshape(width, -1)
    down_out[...] = down
    branch_low = branch[...]
    grad_hidden = (dot(branch_low, down) * slope[...]).astype(LOW)
    hidden_out[...] = grad_hidden
    grad_two = dot(grad_hidden, up[...], 1, 1)
    scaled, rate = norm_stats(middle[...])
    back = norm_back(grad_two, scaled, rate, vectors[1:2])
    low = back.astype(LOW)
    low_out[...] = low
    rows = keep.shape[1]
    keep[0] = fold_rows(dot(low, proj[0]) + dot(branch_low, proj[0]))
    keep[1] = fold_rows(dot(low, proj[2]))
    near[:rows, :] = fold_rows(dot(low, proj[1])).astype(LOW)
    near[rows : 2 * rows, :] = fold_rows(dot(low, proj[3])).astype(LOW)
    first_tp = jnp.where(lax.axis_index("tp") == 0, 1.0, 0.0)
    attn = (back + first_tp * branch_low.astype(F32)).astype(LOW)
    blocks = (mixed[...], paired[:rows, :], mixed_far[...], paired[rows : 2 * rows, :])
    grads = [
        dot(attn, unfold_rows(block.astype(F32), attn.shape[0]).astype(LOW), 0, 0)
        for block in blocks
    ]
    near[2 * rows :, :] = wide([grads[1], grads[3]]).astype(LOW)
    proj_keep[...] = wide([grads[0], grads[2]])
    branch_sum = jnp.sum(branch_low.astype(F32), axis=0, keepdims=True) * first_tp
    sums[...] = jnp.concatenate(
        [
            jnp.sum(grad_two * scaled, axis=0, keepdims=True),
            jnp.sum(grad_two, axis=0, keepdims=True),
            branch_sum + jnp.sum(back, axis=0, keepdims=True),
            branch_sum,
            jnp.sum(grad_hidden.astype(F32), axis=0, keepdims=True),
            jnp.zeros((3, sums.shape[1]), F32),
        ],
        axis=0,
    )


def up_grads_body(n, two, hidden, sent, kept):
    kept[...] = dot(two[...], hidden[...], 0, 0)
    give(n, kept, sent)


def ffn_rows_body(gelu, branch, low, middle, down, near, keep, own_middle, own_branch, chunks):
    rows = own_middle.shape[0]
    chunks[:, rows - 2 :, :] = jnp.zeros_like(chunks[:, rows - 2 :, :])
    to_chunks(dot(gelu[...], down[...], 1, 1), chunks)
    near[0] = chunks[1].astype(LOW)
    near[1] = chunks[3].astype(LOW)
    keep[0] = chunks[0]
    keep[2] = chunks[2]
    to_chunks(low[...].astype(F32), chunks)
    near[2] = chunks[1].astype(LOW)
    near[3] = chunks[3].astype(LOW)
    keep[1] = chunks[0]
    keep[3] = chunks[2]
    to_chunks(middle[...], chunks)
    own_middle[...] = chunks[0, :rows, :]
    to_chunks(branch[...].astype(F32), chunks)
    own_branch[...] = chunks[0, :rows, :]


def rows_body(counts, rows_own, far, own_middle, own_branch, vectors, layer_out, middle_grad):
    own, _ = own_other(counts)
    rows = layer_out.shape[0]
    ids = lax.broadcasted_iota(jnp.int32, (rows, 1), 0) + lax.axis_index("tp") * rows
    mlp = rows_own[0] + far[0].astype(F32)
    value = own_middle[...] + mlp[:rows] + vectors[5:6]
    layer_out[...] = jnp.where(ids < own, value, 0.0).astype(LOW)
    back = rows_own[1] + far[1].astype(F32)
    middle_grad[...] = own_branch[...] + back[:rows]


def attend_back_body(
    back, far, q, k, v, e, scales, turned, weights, act, other, sums_in,
    row_near, own_out, other_out, near, keep, own_act, sums, chunks,
):
    slots, hw = q.shape
    grad_mixed = back[...] + far[...].astype(F32)
    grad_mixed = unfold_rows(grad_mixed, slots).astype(LOW).astype(F32)
    scaled_grads = [
        grad_mixed[:, h * HD : (h + 1) * HD] * scales[:, h : h + 1] for h in range(hw // HD)
    ]
    scaled_grad = wide(scaled_grads)
    inner = scaled_grad.T * turned[...]
    scaled_low = scaled_grad.astype(LOW)
    scale = 1.0 / math.sqrt(HD)
    gq, gk, gv = [], ([], []), ([], [])
    for h in range(hw // HD):
        cols = slice(h * HD, (h + 1) * HD)
        grad = scaled_low[:, cols]
        row = jnp.sum(inner[cols], axis=0, keepdims=True)
        gq_head = 0.0
        for i in range(2):
            gv[i].append(dot(e[h, i], grad))
            probs_grad = dot(v[i][:, cols], grad, 1, 1)
            scores_grad = (e[h, i].astype(F32) * (probs_grad - row)).astype(LOW)
            gk[i].append(dot(scores_grad, q[:, cols]))
            gq_head = gq_head + dot(k[i][:, cols], scores_grad, 0, 0)
        gq.append(gq_head * scale)
    gq = jnp.concatenate(gq, axis=0).T
    own_out[...] = wide([gq, *gk[0], *gv[0]]).astype(LOW)
    other_out[...] = wide([*gk[1], *gv[1]]).astype(LOW)
    rows = own_act.shape[0]
    chunks[:, rows - 2 :, :] = jnp.zeros_like(chunks[:, rows - 2 :, :])
    near[4:] = row_near[...]
    gain_sum, shift_sum = 0.0, 0.0
    for i, src in enumerate((act, other)):
        if i == 0:
            grad = dot(own_out[...], weights[:, : 3 * hw], 1, 1)
        else:
            grad = dot(other_out[...], weights[:, hw : 3 * hw], 1, 1)
        scaled, _ = norm_stats(src[...].astype(F32))
        gain_sum = gain_sum + jnp.sum(grad * scaled, axis=0, keepdims=True)
        shift_sum = shift_sum + jnp.sum(grad, axis=0, keepdims=True)
        to_chunks(grad, chunks)
        near[2 * i] = chunks[1].astype(LOW)
        near[2 * i + 1] = chunks[3].astype(LOW)
        keep[2 * i] = chunks[0]
        keep[2 * i + 1] = chunks[2]
    to_chunks(act[...].astype(F32), chunks)
    own_act[...] = chunks[0, :rows, :]
    ones = jnp.ones((8, slots), LOW)
    own_sums = dot(ones, own_out[...])[0:1]
    other_sums = dot(ones, other_out[...])[0:1]
    head_v = own_sums[:, 2 * hw :] + other_sums[:, hw:]
    pad = jnp.zeros((1, sums.shape[1] - 2 * hw), F32)
    sums[...] = jnp.concatenate(
        [
            gain_sum,
            sums_in[0:1],
            shift_sum,
            sums_in[1:2],
            sums_in[2:3],
            sums_in[3:4],
            sums_in[4:5],
            wide([own_sums[:, :hw], head_v, pad]),
        ],
        axis=0,
    )


def head_grads_body(
    n, own, other, normed_own, normed_other, proj_own, proj_far, sent, early, kept
):
    hw = own.shape[1] // 3
    far = jnp.concatenate([proj_far[:, :hw], proj_far[:, hw:]], axis=0)
    from_own = dot(normed_own[...], own[...], 0, 0)
    from_other = dot(normed_other[...], other[...], 0, 0)
    k_grad = from_own[:, hw : 2 * hw] + from_other[:, :hw]
    v_grad = from_own[:, 2 * hw :] + from_other[:, hw:]
    kept[...] = wide([from_own[:, :hw], k_grad, v_grad, proj_own[...] + far.astype(F32)])
    give(n, kept, sent)
    early[...] = sent[:, : early.shape[1]]


def head_late_body(sent, sums, late):
    rows, half = sent.shape[0], late.shape[1]
    late[:rows, :] = sent[:, half:]
    packed = split_sums(sums[...])
    late[rows : rows + 16, :] = packed[:, :half]
    late[rows + 16 :, :] = packed[:, half:]


def head_first_body(n, value, early, late, sums, got, both, out):
    rows = early.shape[0]
    got[...] = wide([early[...], late[:rows, :]])
    both[...] = sums[...] + joined_sums(wide([late[rows : rows + 16, :], late[rows + 16 :, :]]))
    half = value.shape[0] // n // 2
    ring_first_body(n, value, got, out.at[:half, :])
    out[half:, :] = split_sums(both[...])


def swap_end_body(mine, other, grad):
    grad[...] = mine[...] + other[...].astype(F32)


def tp_sums_body(own, near, out):
    shared = lax.broadcasted_iota(jnp.int32, own.shape, 0) < 6
    out[...] = own[...] + jnp.where(shared, near[...], 0.0)


def finish_body(n, mine, other, sums, qkv_grad, proj_grad, gains, biases, heads, hidden):
    shard = lax.axis_index("shard")
    rows = mine.shape[0]
    total = mine[...] + other[:rows, :].astype(F32)
    hw = proj_grad.shape[0]
    for i in range(3):
        qkv_grad[i] = total[:, i * hw : (i + 1) * hw]
    proj_grad[...] = total[:, 3 * hw :].T
    shared = sums[...] + joined_sums(other[rows:, :])
    part = gains.shape[1]
    own = 0.0
    for g in range(n):
        own = own + jnp.where(shard == g, shared[:, g * part : (g + 1) * part], 0.0)
    gains[...] = own[0:2]
    biases[...] = own[2:6]
    hidden[...] = shared[6]
    heads[...] = jnp.concatenate([shared[7:8, :hw], shared[7:8, hw : 2 * hw]], axis=0)


def halfway_body(keep, row_keep, near, own, far, rows_own, rows_far):
    own[0] = keep[0] + near[0].astype(F32)
    own[1] = keep[2] + near[2].astype(F32)
    far[0] = (keep[1] + near[1].astype(F32)).astype(LOW)
    far[1] = (keep[3] + near[3].astype(F32)).astype(LOW)
    rows_own[0] = row_keep[0] + near[4].astype(F32)
    rows_own[1] = row_keep[1] + near[6].astype(F32)
    rows_far[0] = (row_keep[2] + near[5].astype(F32)).astype(LOW)
    rows_far[1] = (row_keep[3] + near[7].astype(F32)).astype(LOW)


def input_cross_body(own, far, kept, out):
    kept[...] = own[0] + far[0].astype(F32)
    out[...] = (own[1] + far[1].astype(F32)).astype(LOW)


def input_body(kept, cross, own_act, middle_grad, vectors, out):
    rows = out.shape[0]
    grad = kept[...] + cross[...].astype(F32)
    scaled, rate = norm_stats(own_act[...])
    back = norm_back(grad[:rows], scaled, rate, vectors[0:1])
    out[...] = (middle_grad[...] + back).astype(LOW)


def per_device(
    activations,
    slot_counts,
    qkv_weight,
    proj_weight,
    up_weight,
    down_weight,
    norm_gains,
    row_biases,
    head_biases,
    hidden_bias,
    cotangent,
):
    images, slots, width = activations.shape
    n = lax.axis_size("shard")
    n_ctx = lax.axis_size("ctx")
    n_tp = lax.axis_size("tp")
    assert images == 1 and n_ctx == 2 and n_tp == 4 and n % 2 == 0
    part = width // n
    hw = qkv_weight.shape[2]
    ff = up_weight.shape[1]
    quarter = slots // n_tp
    padded = (quarter + 7) // 8 * 8
    fold = folded_rows(slots)
    heads = hw // HD

    now = None

    def place(x):
        nonlocal now
        if now is not None:
            x, now = lax.optimization_barrier((x, now))
        return x

    def wait(*arrays):
        nonlocal now
        now, *arrays = lax.optimization_barrier((now, *arrays))
        return arrays[0] if len(arrays) == 1 else arrays

    def run(body, name, out, args, scalars=0, scratch=(), room=24, weight=0):
        nonlocal now
        outs = call(body, name, out, args, scalars, scratch, room, now, weight)
        now = outs[-1]
        return outs if len(outs) > 1 else outs[0]

    def move(x, axes, moves):
        return lax.ppermute(place(x), axes, moves)

    def over_ctx(x):
        return move(x, "ctx", [(i, i ^ 1) for i in range(n_ctx)])

    def over_tp(x, bit):
        return move(x, "tp", [(i, i ^ bit) for i in range(n_tp)])

    def ring(x):
        moves = [
            (i * n_ctx + r, ((i + (1 if r == 0 else n - 1)) % n) * n_ctx + r)
            for i in range(n)
            for r in range(n_ctx)
        ]
        return move(x, ("shard", "ctx"), moves)

    def step(x, k):
        return move(x, "shard", [(i, (i + k) % n) for i in range(n)])

    def with_n(body, *more):
        return functools.partial(body, n, *more)

    far = n // 2

    def first_hops(block):
        parts, x = [block], ring(block)
        for _ in range(far - 2):
            x = wait(x)
            parts += [x, over_ctx(x)]
            x = ring(x)
        return parts, x

    def half_of(x, weight=0):
        size = (x.shape[0] // 2, x.shape[1])
        return run(half_body, "half", [shape(size)], [x], weight=weight)

    def mark(x, weight):
        run(mark_body, "mark", [shape((8, 128), F32)], [x], weight=weight)

    def ring_step(weight, left, kept, got, came, *sums):
        cols = kept.shape[1]
        extra = 16 * len(sums)
        return run(
            with_n(ring_step_body, left, extra),
            "ring_step",
            [shape((part + extra, cols))],
            [kept, got, came, *sums],
            weight=weight,
        )

    act = activations[0]
    down_turned = down_weight.T
    rows = -(-(part + 6) // 32) * 32
    pack, pack_half, act_half = run(
        pack_body,
        "pack",
        [shape((rows, width)), shape((rows // 2, width)), shape((slots, width // 2))],
        [qkv_weight, norm_gains, row_biases, proj_weight, act],
        room=58,
    )
    pack_parts, last = first_hops(pack)
    piece = step(pack_half, far)
    act_far = over_ctx(act_half)
    last = wait(last)
    mark(last, 0)
    pack_parts += [last, over_ctx(last)]
    up_parts, up_last = first_hops(up_weight)
    act_far = wait(act_far)
    act_near = over_tp(act_far, 1)
    piece = wait(piece)
    mark(piece, 20)
    pack_parts += [piece, over_ctx(piece)]
    pack_parts[-3] = wait(pack_parts[-3])
    up_last = wait(up_last)
    up_piece = half_of(up_last)
    up_piece = ring(up_piece)
    up_parts += [up_last, over_ctx(up_last)]
    weights, proj, vectors, other = run(
        with_n(join_body),
        "join",
        [
            shape((width, width)),
            shape((width // 2, 2 * hw)),
            shape((8, width), F32),
            shape((slots, width)),
        ],
        [act_far, act_near, *pack_parts],
        scratch=[pltpu.VMEM((n, rows, width), LOW)],
        weight=20,
    )
    proj_far = over_tp(proj, 2)
    down_parts, down_last = first_hops(down_turned)
    (mixed, turned, scales, normed_own, normed_other, q, k, v, e) = run(
        attend_body,
        "attend",
        [
            shape((fold, 2 * hw)),
            shape((hw, slots), F32),
            shape((slots, 8), F32),
            shape((slots, width)),
            shape((slots, width)),
            shape((slots, hw)),
            shape((2, slots, hw)),
            shape((2, slots, hw)),
            shape((heads, 2, slots, slots)),
        ],
        [slot_counts, act, other, weights, vectors, head_biases],
        scalars=1,
    )
    mixed_far = over_tp(mixed, 2)
    up_piece = wait(up_piece)
    up_parts += [up_piece, over_ctx(up_piece)]
    up_parts[-3] = wait(up_parts[-3])
    mark(up_parts[-3], 3)
    proj_far = wait(proj_far)
    down_last = wait(down_last)
    mixed_far = wait(mixed_far)
    paired = run(
        pair_body,
        "pair",
        [shape((2 * fold + width, 2 * hw))],
        [mixed, mixed_far, proj, proj_far],
    )
    paired = over_tp(paired, 1)
    up_parts[-1] = wait(up_parts[-1])
    down_piece = half_of(down_last, 10)
    down_piece = ring(down_piece)
    down_parts += [down_last, over_ctx(down_last)]
    two, gelu, slope, branch, middle, up, proj_full = run(
        with_n(hidden_body),
        "hidden",
        [
            shape((slots, width)),
            shape((slots, ff)),
            shape((slots, ff), F32),
            shape((slots, width)),
            shape((slots, width), F32),
            shape((width, ff)),
            shape((n_tp, width, hw)),
        ],
        [slot_counts, act, mixed, mixed_far, proj, proj_far, paired, vectors]
        + [hidden_bias.reshape(1, ff), cotangent[0]]
        + up_parts,
        scalars=1,
        scratch=[pltpu.VMEM((n, part, ff), LOW)],
    )
    down_piece = wait(down_piece)
    down_parts += [down_piece, over_ctx(down_piece)]
    down_total, to_up, to_down = run(
        with_n(down_grads_body),
        "down_grads",
        [shape((width, ff), F32)] + [shape((part // 2, ff))] * 2,
        [branch, gelu],
    )
    to_up, to_down = step(to_up, 1), step(to_down, n - 1)
    near, keep, proj_keep, hidden, back_low, down, sums = run(
        with_n(middle_back_body),
        "middle_back",
        [
            shape((2 * fold + width, 2 * hw)),
            shape((2, fold, 2 * hw), F32),
            shape((width, 2 * hw), F32),
            shape((slots, ff)),
            shape((slots, width)),
            shape((width, ff)),
            shape((8, width), F32),
        ],
        [branch, slope, up, middle, vectors, proj_full, mixed, mixed_far, paired] + down_parts,
        scratch=[pltpu.VMEM((n, part, ff), LOW)],
    )
    near = over_tp(near, 1)
    up_sent, up_kept = run(
        with_n(up_grads_body),
        "up_grads",
        [shape((far * part, ff)), shape((width, ff), F32)],
        [two, hidden],
    )
    for left in range(far - 1, 0, -1):
        to_up, to_down = wait(to_up, to_down)
        to_up, to_down = run(
            with_n(both_ways_body, left),
            "both_ways",
            [shape((part, ff))] * 2,
            [down_total, to_up, to_down],
            weight=20,
        )
        if left > 1:
            to_up, to_down = step(to_up, 1), step(to_down, n - 1)
    near = wait(near)
    back, proj_own, back_far, proj_far = run(
        add_body,
        "back_add",
        [
            shape((fold, 2 * hw), F32),
            shape((width, hw), F32),
            shape((fold, 2 * hw)),
            shape((width // 2, 2 * hw)),
        ],
        [keep, proj_keep, near],
    )
    back_far = over_tp(back_far, 2)
    proj_far = over_tp(proj_far, 2)
    to_up, to_down = step(to_up, 1), step(to_down, n - 1)
    up_got = over_ctx(up_sent)
    row_near, row_keep, own_middle, own_branch = run(
        ffn_rows_body,
        "ffn_rows",
        [
            shape((4, padded, width)),
            shape((4, padded, width), F32),
            shape((quarter, width), F32),
            shape((quarter, width), F32),
        ],
        [gelu, branch, back_low, middle, down],
        scratch=[pltpu.VMEM((n_tp, padded, width), F32)],
    )
    back_far = wait(back_far)
    mark(back_far, 60)
    own_grads, other_grads, near, keep, own_act, sums = run(
        attend_back_body,
        "attend_back",
        [
            shape((slots, 3 * hw)),
            shape((slots, 2 * hw)),
            shape((8, padded, width)),
            shape((4, padded, width), F32),
            shape((quarter, width), F32),
            shape((8, width), F32),
        ],
        [back, back_far, q, k, v, e, scales, turned, weights, act, other, sums, row_near],
        scratch=[pltpu.VMEM((n_tp, padded, width), F32)],
    )
    to_up, to_down = wait(to_up, to_down)
    down_mine, down_low = run(
        with_n(both_ways_end_body),
        "both_ways_end",
        [shape((part, ff), F32), shape((part, ff))],
        [down_total, to_up, to_down],
    )
    proj_far = wait(proj_far)
    head_sent, head_early, head_kept = run(
        with_n(head_grads_body),
        "head_grads",
        [shape((far * part, width)), shape((far * part, width // 2)), shape((width, width), F32)],
        [own_grads, other_grads, normed_own, normed_other, proj_own, proj_far],
    )
    head_early = over_ctx(head_early)
    sums_near = over_tp(sums, 1)
    near = over_tp(near, 1)
    sums_near = wait(sums_near)
    sums = run(tp_sums_body, "tp_sums", [shape((8, width), F32)], [sums, sums_near])
    sums_far = over_tp(sums, 2)
    up_got = wait(up_got)
    up_came = run(
        with_n(ring_first_body),
        "ring_first",
        [shape((part // 2, ff))],
        [up_kept, up_got],
        weight=30,
    )
    up_came = ring(up_came)
    sums_far = wait(sums_far)
    sums = run(tp_sums_body, "tp_sums", [shape((8, width), F32)], [sums, sums_far])
    head_late = run(
        head_late_body,
        "head_late",
        [shape((far * part + 32, width // 2))],
        [head_sent, sums],
    )
    head_late = over_ctx(head_late)
    down_other = over_ctx(down_low)
    near = wait(near)
    input_own, input_far, rows_own, rows_far = run(
        halfway_body,
        "halfway",
        [shape((2, padded, width), F32), shape((2, padded, width))] * 2,
        [keep, row_keep, near],
    )
    input_far = over_tp(input_far, 2)
    head_early = wait(head_early)
    for left in range(far - 1, 0, -1):
        up_came = wait(up_came)
        up_came = ring(ring_step(20, left, up_kept, up_got, up_came))
    head_late = wait(head_late)
    head_got, sums, head_came = run(
        with_n(head_first_body),
        "head_first",
        [shape((far * part, width)), shape((8, width), F32), shape((part // 2 + 16, width))],
        [head_kept, head_early, head_late, sums],
    )
    head_came = ring(head_came)
    rows_far = over_tp(rows_far, 2)
    input_far = wait(input_far)
    input_kept, input_cross = run(
        input_cross_body,
        "input_cross",
        [shape((padded, width), F32), shape((padded, width))],
        [input_own, input_far],
    )
    input_cross = over_ctx(input_cross)
    up_came = wait(up_came)
    up_mine, up_low = run(
        with_n(ring_end_body, 0),
        "up_end",
        [shape((part, ff), F32), shape((part, ff))],
        [up_kept, up_got, up_came],
    )
    up_other = over_ctx(up_low)
    down_other = wait(down_other)
    down_grad = run(
        swap_end_body, "swap_end", [shape((part, ff), F32)], [down_mine, down_other], weight=40
    )
    for left in range(far - 1, 0, -1):
        head_came = wait(head_came)
        head_came = ring(ring_step(0, left, head_kept, head_got, head_came, sums))
    head_came = wait(head_came)
    head_mine, head_low, sums = run(
        with_n(ring_end_body, 1),
        "ring_end",
        [shape((part, width), F32), shape((part + 16, width)), shape((8, width), F32)],
        [head_kept, head_got, head_came, sums],
    )
    head_other = over_ctx(head_low)
    input_cross = wait(input_cross)
    mark(input_cross, 40)
    rows_far = wait(rows_far)
    layer_out, middle_grad = run(
        rows_body,
        "rows",
        [shape((quarter, width)), shape((quarter, width), F32)],
        [slot_counts, rows_own, rows_far, own_middle, own_branch, vectors],
        scalars=1,
    )
    input_grad = run(
        input_body,
        "input",
        [shape((quarter, width))],
        [input_kept, input_cross, own_act, middle_grad, vectors],
    )
    up_other = wait(up_other)
    up_grad = run(swap_end_body, "swap_end", [shape((part, ff), F32)], [up_mine, up_other])
    qkv_grad, proj_grad, gains_grad, biases_grad, heads_grad, hidden_grad = run(
        with_n(finish_body),
        "finish",
        [
            shape((3, part, hw), F32),
            shape((hw, part), F32),
            shape((2, part), F32),
            shape((4, part), F32),
            shape((2, hw), F32),
            shape((ff,), F32),
        ],
        [head_mine, head_other, sums],
    )
    return (
        layer_out[None],
        input_grad[None],
        qkv_grad,
        proj_grad,
        up_grad,
        down_grad.T,
        gains_grad,
        biases_grad,
        heads_grad,
        hidden_grad,
    )


def solution(mesh):
    placed = (
        P("shard", "ctx", None),
        P("shard", None),
        P(None, "shard", "tp"),
        P("tp", "shard"),
        P("shard", "tp"),
        P("tp", "shard"),
        P(None, "shard"),
        P(None, "shard"),
        P(None, "tp"),
        P("tp"),
        P("shard", "ctx", None),
    )
    return jax.shard_map(
        per_device,
        mesh=mesh,
        in_specs=placed,
        out_specs=(
            P("shard", ("ctx", "tp"), None),
            P("shard", ("ctx", "tp"), None),
            P(None, "shard", "tp"),
            P("tp", "shard"),
            P("shard", "tp"),
            P("tp", "shard"),
            P(None, "shard"),
            P(None, "shard"),
            P(None, "tp"),
            P("tp"),
        ),
        check_vma=False,
    )
```
